256 devices in a mesh: dom: 128 (over x, y, z), feat: 2 (over core).
Axes of the slice: x: 4, y: 4, z: 8, core: 2. Of those that a mesh axis runs over, the one named last changes fastest.
Arguments:
- increments: bfloat16 [524288, 128], P('dom'), may hold values from -6 to 6
- w_in: bfloat16 [128, 256], replicated, may hold values from -0.5 to 0.5
- w_node1: bfloat16 [512, 512], replicated, may hold values from -0.25 to 0.25
- w_node2: bfloat16 [512, 256], replicated, may hold values from -0.25 to 0.25
- w_out: bfloat16 [256, 128], replicated, may hold values from -0.375 to 0.375
- grid_edges: int32 [131072, 4], P('dom'), may hold values from 0 to 4095
- mesh_edges: int32 [131072, 6], P('dom'), may hold values from 0 to 3071
- mesh_mask: int32 [131072, 6], P('dom'), may hold values 0 or 1
- send_rows: int32 [128, 128, 16], P('dom'), may hold values from 0 to 1023
- site_owner: int32 [32768, 1], P('dom'), may hold values from 0 to 127; in each aligned block of 256 rows (0 to 255, 256 to 511, ...) at most 4 rows name the same one
- site_nodes: int32 [32768, 8], P('dom'), may hold values from 0 to 1023
- site_obs: bfloat16 [32768, 128], P('dom'), may hold values from -4 to 4
Outputs:
- grad_grid: float32 [524288, 128], P('dom', 'feat')
- site_pred: bfloat16 [32768, 128], P('dom')
The draws below stay inside these ranges and needn't reach their ends.
Inputs may be any that keep to these rules, and one draw needn't show every extreme that they name: `site_owner`: among the rows of one partition, at most 4 sites name the same owner, and that many do in some partition.
All inputs are finite; a program needn't handle non-finite values. No bound on the sum of `mesh_mask` on one device may be relied on, other than what follows from the above.
Results may differ from the reference program's by a relative error of at most 0.012.
Values may be sent and summed in bfloat16 or wider, within the bound.
No kernel may reach another device: no remote copies, remote signals or barrier semaphores. Data moves between devices by JAX's collectives and lax.ppermute only.
A program may use at most 64 MiB of HBM per device.

```python
import math
import jax
import jax.numpy as jnp
import numpy as np
from jax import lax

H = 256
F = 512
C = 128
G_DEV = 4096
M_DEV = 1024
S_DEV = 256
KE = 4
K = 6
KS = 8
R = 16
CAP = 4
GRID = 524288
MESH = 131072
SITES = 32768
N_DOM = 128


def set_ends(result, key, low, largest):
    extent = result.shape
    spot = [jax.random.randint(jax.random.fold_in(key, axis), (), 0, extent[axis]) for axis in range(len(extent))]
    result = result.at[tuple(spot)].set(low)
    longest = extent.index(max(extent))
    spot[longest] = (spot[longest] + 1) % extent[longest]
    return result.at[tuple(spot)].set(largest)


def shard_levels(stream_key, shape, pieces, smallest, high):
    def one(axis_at, shards_of):
        steps = jax.random.uniform(jax.random.fold_in(jax.random.fold_in(stream_key, 6), axis_at), (shards_of,), jnp.float32, smallest / len(pieces), high / len(pieces))
        return jnp.repeat(jnp.exp(steps), shape[axis_at] // shards_of).reshape((-1,) + (1,) * (len(shape) - axis_at - 1))

    factor_of = one(*pieces[0])
    for cut in pieces[1:]:
        factor_of = factor_of * one(*cut)
    return factor_of


def shared_out(own_key, own, number, rows, number_of, top, bound, skew):
    order = jax.random.permutation(own_key, number_of)
    crowded, usual = shares(number_of, rows * top, bound, skew, True), shares(number_of, rows * top, bound, skew, False)
    places = jnp.arange(number_of)

    def named(lengths, offset_by):
        used = int((lengths > 0).sum())
        fixed = max(1, used // 4)
        passed = fixed + (places - fixed + offset_by * (used - fixed)) % max(1, number_of - fixed)
        return jnp.zeros((number_of,), jnp.int32).at[order[jnp.where(places < fixed, places, passed)]].set(jnp.asarray(lengths, jnp.int32))

    lengths = jnp.where(number % 4 == 0, named(crowded, number // 4), named(usual, number - number // 4 - 1))
    mixed = jax.random.permutation(jax.random.fold_in(own, 3), number_of)
    source_of, receiver = mixed[0:number_of // 2 * 2:2], mixed[1:number_of // 2 * 2:2]
    room = jnp.minimum(lengths[source_of] - 1, bound - lengths[receiver]) // 2
    room = jnp.where((source_of == order[0]) | (receiver == order[0]) | (lengths[receiver] == 0), 0, jnp.maximum(room, 0))
    passed = jax.random.randint(jax.random.fold_in(own, 4), (number_of // 2,), 0, 1 << 20) % (room + 1)
    lengths = lengths.at[source_of].add(-passed).at[receiver].add(passed)
    items = jnp.searchsorted(jnp.cumsum(lengths), jnp.arange(rows * top), side="right").astype(jnp.int32)
    table = items.reshape(top, rows).T
    table = table[jax.random.permutation(jax.random.fold_in(own, 1), rows)]
    offset_by = jax.random.randint(jax.random.fold_in(own, 2), (rows, 1), 0, top)
    return jnp.take_along_axis(table, (jnp.arange(top)[None, :] + offset_by) % top, axis=1)


def shares(count, total, most, skew, full):
    weights = [(1 << 20) // math.isqrt(standing ** skew) + 1 for standing in range(1, count + 1)]
    largest = most if full else min(most, max(-(-total // count), total * weights[0] // sum(weights)))
    least = 1 if total - largest >= count - 1 else 0
    given, spare = [largest] + [least] * (count - 1), total - largest - least * (count - 1)
    while spare > 0:
        free = [i for i in range(1, count) if given[i] < largest] or [i for i in range(1, count) if given[i] < most]
        whole, left = sum([weights[i] for i in free]), spare
        for i in free:
            more = min(most - given[i], max(1, left * weights[i] // whole), spare)
            given[i] = given[i] + more
            spare = spare - more
    return np.array(given)


def normal_values(stream_key, shape, scale, reach, shards=(), kind=jnp.bfloat16):
    drawn = jax.random.normal(stream_key, shape, jnp.float32) * scale
    if len(shards) > 0:
        drawn = shard_levels(stream_key, shape, shards, -0.22, 0.18) * drawn
    return jnp.clip(drawn, min=-reach, max=reach).astype(kind)


def setup_inputs(seed: int = 0) -> dict:
    streams_of = jax.random.split(jax.random.key(seed), 13)
    increments = normal_values(streams_of[0], (GRID, C), 1.0, 6.0, ((0, 128),))
    w_in = normal_values(streams_of[1], (C, H), C ** -0.5, 0.5)
    w_node1 = normal_values(streams_of[2], (2 * H, F), (2 * H) ** -0.5, 0.25)
    w_node2 = normal_values(streams_of[3], (F, H), F ** -0.5, 0.25)
    w_out = normal_values(streams_of[4], (H, C), H ** -0.5, 0.375)
    grid_edges = set_ends(jax.random.randint(streams_of[5], (MESH, KE), 0, G_DEV), jax.random.fold_in(streams_of[5], 1), 0, G_DEV - 1).astype(jnp.int32)
    mesh_edges = set_ends(jax.random.randint(streams_of[6], (MESH, K), 0, M_DEV + N_DOM * R), jax.random.fold_in(streams_of[6], 1), 0, (M_DEV + N_DOM * R) - 1).astype(jnp.int32)
    mesh_mask = set_ends((jax.random.randint(streams_of[7], (MESH, K), 0, 4) < 3).astype(jnp.int32), jax.random.fold_in(streams_of[7], 1), 0, 1)
    send_rows = set_ends(jax.random.randint(streams_of[8], (N_DOM, N_DOM, R), 0, M_DEV), jax.random.fold_in(streams_of[8], 1), 0, M_DEV - 1).astype(jnp.int32)
    site_owner_keys = jax.random.split(jax.random.fold_in(streams_of[9], 1), SITES // S_DEV)
    site_owner_turns = jax.random.permutation(jax.random.fold_in(streams_of[9], 3), SITES // S_DEV)
    site_owner = jax.vmap(lambda own, number: shared_out(jax.random.fold_in(streams_of[9], 2), own, number, S_DEV, N_DOM, 1, CAP, 2))(site_owner_keys, site_owner_turns).reshape((SITES, 1))
    site_nodes = set_ends(jax.random.randint(streams_of[10], (SITES, KS), 0, M_DEV), jax.random.fold_in(streams_of[10], 1), 0, M_DEV - 1).astype(jnp.int32)
    site_obs = normal_values(streams_of[11], (SITES, C), 0.3, 4.0, ((0, 128),))
    return dict(increments=increments, w_in=w_in, w_node1=w_node1, w_node2=w_node2, w_out=w_out, grid_edges=grid_edges, mesh_edges=mesh_edges, mesh_mask=mesh_mask, send_rows=send_rows, site_owner=site_owner, site_nodes=site_nodes, site_obs=site_obs)


def silu_slope(pre):
    sig = jax.nn.sigmoid(pre)
    return sig * (1.0 + pre * (1.0 - sig))


def reference(increments, w_in, w_node1, w_node2, w_out, grid_edges, mesh_edges, mesh_mask, send_rows, site_owner, site_nodes, site_obs):
    domains = N_DOM
    mesh_total = M_DEV * domains

    def encode(args):
        grid_block, edge_block = args
        embedded = jnp.dot(grid_block, w_in, preferred_element_type=jnp.float32).astype(jnp.bfloat16)
        return (jnp.sum(embedded[edge_block].astype(jnp.float32), axis=1) / KE).astype(jnp.bfloat16)

    latent = lax.map(encode, (increments.reshape(domains, G_DEV, C), grid_edges.reshape(domains, M_DEV, KE)))
    owners = jnp.broadcast_to(jnp.arange(domains, dtype=jnp.int32)[None, :, None], (domains, domains, R))
    halo_rows = jnp.swapaxes(send_rows, 0, 1)
    halo = latent[owners, halo_rows].reshape(domains, domains * R, H)
    edges = mesh_edges.reshape(domains, M_DEV, K)
    weights = mesh_mask.reshape(domains, M_DEV, K).astype(jnp.float32)

    def mix(latent_block, halo_block, edge_block, weight_block):
        extended = jnp.concatenate([latent_block, halo_block], axis=0)
        aggregate = jnp.sum(extended[edge_block].astype(jnp.float32) * weight_block[:, :, None], axis=1).astype(jnp.bfloat16)
        pre = jnp.dot(latent_block, w_node1[:H], preferred_element_type=jnp.float32) + jnp.dot(aggregate, w_node1[H:], preferred_element_type=jnp.float32)
        return pre

    def forward(args):
        latent_block, halo_block, edge_block, weight_block = args
        pre = mix(latent_block, halo_block, edge_block, weight_block)
        hidden = jax.nn.silu(pre).astype(jnp.bfloat16)
        return (latent_block.astype(jnp.float32) + jnp.dot(hidden, w_node2, preferred_element_type=jnp.float32)).astype(jnp.bfloat16)

    latent_next = lax.map(forward, (latent, halo, edges, weights)).reshape(mesh_total, H)
    site_rows = (site_owner[:, 0:1] * M_DEV + site_nodes).astype(jnp.int32)

    def readout(rows):
        pooled = jnp.sum(latent_next[rows].astype(jnp.float32), axis=1).astype(jnp.bfloat16)
        return jnp.dot(pooled, w_out, preferred_element_type=jnp.float32)

    values = lax.map(readout, site_rows.reshape(domains, S_DEV, KS)).reshape(S_DEV * domains, C)
    site_pred = values.astype(jnp.bfloat16)
    diff = (values - site_obs.astype(jnp.float32)).astype(jnp.bfloat16)
    pool_grad = jnp.dot(diff, w_out.T, preferred_element_type=jnp.float32)
    next_grad = jnp.zeros((mesh_total, H), jnp.float32)
    for column in range(KS):
        next_grad = next_grad.at[site_rows[:, column]].add(pool_grad)

    def backward(args):
        latent_block, halo_block, edge_block, weight_block, grad_block = args
        pre = mix(latent_block, halo_block, edge_block, weight_block)
        grad_low = grad_block.astype(jnp.bfloat16)
        slope = jnp.dot(grad_low, w_node2.T, preferred_element_type=jnp.float32)
        inner_grad = (slope * silu_slope(pre)).astype(jnp.bfloat16)
        own_grad = jnp.dot(inner_grad, w_node1[:H].T, preferred_element_type=jnp.float32)
        agg_grad = jnp.dot(inner_grad, w_node1[H:].T, preferred_element_type=jnp.float32)
        spread = (agg_grad[:, None, :] * weight_block[:, :, None]).reshape(M_DEV * K, H)
        ext_grad = jax.ops.segment_sum(spread, edge_block.reshape(-1), num_segments=M_DEV + domains * R)
        local = grad_block + own_grad + ext_grad[:M_DEV]
        return local, ext_grad[M_DEV:].reshape(domains, R, H)

    local, halo_grad = lax.map(backward, (latent, halo, edges, weights, next_grad.reshape(domains, M_DEV, H)))
    target = (owners * M_DEV + halo_rows).reshape(-1)
    latent_grad = local.reshape(mesh_total, H).at[target].add(halo_grad.reshape(-1, H))

    def encode_back(args):
        grad_block, edge_block = args
        spread = jnp.broadcast_to((grad_block / KE)[:, None, :], (M_DEV, KE, H)).reshape(M_DEV * KE, H)
        emb_grad = jax.ops.segment_sum(spread, edge_block.reshape(-1), num_segments=G_DEV).astype(jnp.bfloat16)
        return jnp.dot(emb_grad, w_in.T, preferred_element_type=jnp.float32)

    grad_grid = lax.map(encode_back, (latent_grad.reshape(domains, M_DEV, H), grid_edges.reshape(domains, M_DEV, KE)))
    return grad_grid.reshape(G_DEV * domains, C), site_pred
```

```python
import jax
import jax.numpy as jnp
from jax import lax
from jax.experimental import pallas as pl
from jax.experimental.pallas import tpu as pltpu
from jax.sharding import PartitionSpec as P

BF = jnp.bfloat16
F32 = jnp.float32
I16 = jnp.int16
I32 = jnp.int32
LANES = 128
HALF_DEPTH = 8
SLOTS = 4
ROWS = HALF_DEPTH + SLOTS
SWAP = [(0, 1), (1, 0)]


def dot(a, b, ca=1, cb=0):
    return lax.dot_general(a, b, (((ca,), (cb,)), ((), ())), preferred_element_type=F32)


def iota(shape, axis):
    return lax.broadcasted_iota(I32, shape, axis)


def eq_bf16(a, b):
    return jnp.where(a == b, jnp.asarray(1, BF), jnp.asarray(0, BF))


def build_counts(dst, load, rows, width, degree, block=64, row0=0):
    start = iota((block, LANES), 1).astype(I16)

    def row_body(i, carry):
        s = pl.multiple_of(i * block, block)
        a = load(s, block)
        cols = [
            jnp.broadcast_to(a[:, k : k + 1], (block, LANES)).astype(I16) for k in range(degree)
        ]

        def lane_body(w, lanes):
            acc = eq_bf16(cols[0], lanes)
            for k in range(1, degree):
                acc = acc + eq_bf16(cols[k], lanes)
            dst[pl.ds(row0 + s, block), pl.ds(pl.multiple_of(w * LANES, LANES), LANES)] = acc
            return lanes + jnp.asarray(LANES, I16)

        lax.fori_loop(0, width // LANES, lane_body, start, unroll=2)
        return carry

    lax.fori_loop(0, rows // block, row_body, 0)


def place_matrix(rows, cols, transposed):
    shape = (cols, rows) if transposed else (rows, cols)
    r_axis, c_axis = (1, 0) if transposed else (0, 1)
    c = iota(shape, c_axis)
    want = (c & 127) * ROWS + HALF_DEPTH + (c >> 7)
    return jnp.where(iota(shape, r_axis) == want, 1.0, 0.0).astype(BF)


def send_index(feat, send, rows):
    peers = send.shape[0]
    picked = jnp.where(feat == 0, send[:, :HALF_DEPTH], send[:, HALF_DEPTH:])
    peer = iota((peers, 1), 0)
    table = jnp.concatenate([picked >> 5, picked & 31, peer], axis=1).astype(F32).astype(BF)
    row = iota((rows, peers), 0)
    first = iota((rows, peers), 1) * ROWS
    spread = jnp.where((row >= first) & (row < first + ROWS), 1.0, 0.0).astype(BF)
    out = dot(spread, table)
    node = out[:, :HALF_DEPTH] * 32.0 + out[:, HALF_DEPTH : 2 * HALF_DEPTH]
    within = iota((rows, 1), 0).astype(F32) - out[:, 2 * HALF_DEPTH :] * ROWS
    hit = iota((rows, HALF_DEPTH), 1).astype(F32) == within
    index = jnp.sum(jnp.where(hit, node, 0.0), axis=1, keepdims=True)
    return jnp.where(within >= HALF_DEPTH, -1.0, index).astype(I32)


def encode_kernel(
    feat_ref, inc, edges, send, owner, nodes, obs, msg, ginc, target, g_s, r_s, idx_s
):
    feat = feat_ref[0]
    rows = msg.shape[0]
    build_counts(g_s, lambda s, b: edges[pl.ds(s, b), :], ginc.shape[0], inc.shape[0], edges.shape[1])
    idx_s[...] = send_index(feat, send[...], rows)
    build_counts(r_s, lambda s, b: idx_s[pl.ds(s, b), :], rows, ginc.shape[0], 1)
    sites = owner.shape[0]
    own = owner[...]
    member = jnp.where(own == iota((sites, LANES), 1), 1.0, 0.0)
    member_b = member.astype(BF)
    lower = jnp.where(iota((sites, sites), 1) < iota((sites, sites), 0), 1.0, 0.0).astype(BF)
    rank = jnp.sum(dot(lower, member_b) * member, axis=1, keepdims=True)
    target[...] = own * ROWS + HALF_DEPTH + rank.astype(I32)
    slot0 = (2 * feat).astype(F32)
    obs_0 = dot(jnp.where(rank == slot0, member, 0.0).astype(BF), obs[...], 0, 0)
    obs_1 = dot(jnp.where(rank == slot0 + 1.0, member, 0.0).astype(BF), obs[...], 0, 0)
    degree = nodes.shape[1]
    lane = iota((sites, LANES), 1)
    mine = (lane >> 3).astype(F32) == rank
    tile = jnp.where((iota((degree, LANES), 1) & 7) == iota((degree, LANES), 0), 1.0, 0.0).astype(BF)
    n = nodes[...]
    high = dot(((n >> 5) + 1).astype(F32).astype(BF), tile)
    low = dot((n & 31).astype(F32).astype(BF), tile)
    n_high = dot(member_b, jnp.where(mine, high, 0.0).astype(BF), 0, 0)
    n_low = dot(member_b, jnp.where(mine, low, 0.0).astype(BF), 0, 0)
    packed = jnp.concatenate([obs_0, obs_1, n_high, n_low], axis=0).astype(BF)
    site_rows = dot(place_matrix(rows, SLOTS * LANES, False), packed)
    mean = (dot(g_s[...], inc[...]) * (1.0 / edges.shape[1])).astype(BF)
    ginc[...] = mean
    msg[...] = (dot(r_s[...], mean) + site_rows).astype(BF)


def prepare_kernel(
    feat_ref, edges, mask, w_in, w_node1, w_node2, w_out, m_out, w_cat, w_ho, w_io, idx_s
):
    feat = feat_ref[0]
    rows = edges.shape[0]
    half = rows // 2
    e = edges[...]
    own_col = e - feat * half
    h = e - rows
    r = h & 15
    halo_col = half + (h >> 4) * ROWS + (r & 7)
    is_own = (e < rows) & (own_col >= 0) & (own_col < half)
    is_halo = (e >= rows) & ((r >> 3) == feat)
    col = jnp.where(is_own, own_col, jnp.where(is_halo, halo_col, -1))
    idx_s[...] = jnp.where(mask[...] > 0, col, -1)
    build_counts(m_out, lambda s, b: idx_s[pl.ds(s, b), :], rows, m_out.shape[1], edges.shape[1])
    width = w_in.shape[1]
    variables = w_in.shape[0]
    wi = w_in[...]
    w_cat[:variables, :] = dot(wi, w_node1[:width, :]).astype(BF)
    w_cat[variables:, :] = dot(wi, w_node1[width:, :]).astype(BF)
    w_ho[...] = dot(w_node2[...], w_out[...]).astype(BF)
    w_io[...] = dot(wi, w_out[...]).astype(BF)


def mix_kernel(feat_ref, msg, ginc, m, part, node):
    feat = feat_ref[0]
    rows = ginc.shape[0]
    half = rows // 2
    own = ginc[pl.ds(pl.multiple_of(feat * half, half), half), :]
    part[:rows, :] = (dot(m[:, :half], own) + dot(m[:, half:], msg[...])).astype(BF)
    got = dot(place_matrix(msg.shape[0], SLOTS * LANES, True), msg[...])
    part[rows:, :] = got[: 2 * LANES, :].astype(BF)
    node[...] = ((got[2 * LANES : 3 * LANES, :] - 1.0) * 32.0 + got[3 * LANES :, :]).astype(I32)


def site_kernel(node, s_out):
    degree = 8
    for slot in range(SLOTS):
        build_counts(
            s_out,
            lambda s, b, slot=slot: node[pl.ds(s, b), slot * degree : (slot + 1) * degree],
            LANES,
            s_out.shape[1],
            degree,
            row0=slot * LANES,
        )


def node_kernel(
    feat_ref, part, other, ginc, m, s, w_cat, w_ho, w_io, msg, own_t, ext_t, slope_s
):
    feat = feat_ref[0]
    rows, variables = ginc.shape
    half = rows // 2
    gi = ginc[...]
    agg = (part[:rows, :].astype(F32) + other[:rows, :].astype(F32)).astype(BF)
    pre = dot(gi, w_cat[:variables, :]) + dot(agg, w_cat[variables:, :])
    sig = 1.0 / (1.0 + jnp.exp(-pre))
    hidden = (pre * sig).astype(BF)
    slope_s[...] = sig * (1.0 + pre * (1.0 - sig))
    readout = (dot(hidden, w_ho[...]) + dot(gi, w_io[...])).astype(BF)
    sites = s[...]
    values = dot(sites, readout)
    mine = part[rows:, :].astype(F32)
    theirs = other[rows:, :].astype(F32)
    first = jnp.where(feat == 0, mine, theirs)
    second = jnp.where(feat == 0, theirs, mine)
    diff = (values - jnp.concatenate([first, second], axis=0)).astype(BF)
    d_t = dot(diff, sites, 0, 0).astype(BF)
    d = d_t.T
    inner = (dot(d, w_ho[...], 1, 1) * slope_s[...]).astype(BF)
    cols = pl.ds(pl.multiple_of(feat * (variables // 2), variables // 2), variables // 2)
    own_t[...] = dot(w_io[cols, :], d_t) + dot(w_cat[cols, :], inner, 1, 1)
    agg_t = dot(w_cat[variables:, :], inner, 1, 1).astype(BF)
    ext = dot(agg_t, m[...])
    ext_t[...] = ext[:, :half]
    site_rows = dot(place_matrix(msg.shape[0], SLOTS * LANES, False), values.astype(BF))
    msg[...] = (ext[:, half:].T + site_rows).astype(BF)


def scatter_kernel(feat_ref, edges, send, g_out, r_out, idx_s):
    build_counts(
        g_out, lambda s, b: edges[pl.ds(s, b), :], g_out.shape[0], g_out.shape[1], edges.shape[1]
    )
    idx_s[...] = send_index(feat_ref[0], send[...], r_out.shape[0])
    build_counts(r_out, lambda s, b: idx_s[pl.ds(s, b), :], r_out.shape[0], r_out.shape[1], 1)


def return_kernel(feat_ref, msg, r, ext_t, own_t, target, keep, give, pred, part_s):
    feat = feat_ref[0]
    back = msg[...]
    half = ext_t.shape[1]
    part = dot(back, r[...], 0, 0)
    e = ext_t[...]
    lane = iota(part.shape, 1)
    inside = (lane >= feat * half) & (lane < feat * half + half)
    part_s[...] = part + jnp.where(inside, jnp.concatenate([e, e], axis=1), 0.0)
    n = keep.shape[0]
    keep[...] = part_s[pl.ds(pl.multiple_of(feat * n, n), n), :] + own_t[...]
    give[...] = part_s[pl.ds(pl.multiple_of((1 - feat) * n, n), n), :].astype(BF)
    pick = jnp.where(target[...] == iota((target.shape[0], msg.shape[0]), 1), 1.0, 0.0).astype(BF)
    pred[...] = dot(pick, back).astype(BF)


def grid_kernel(keep, got, g, out, *, degree):
    lg = ((keep[...] + got[...].astype(F32)) * (1.0 / degree)).astype(BF)
    out[...] = dot(lg, g[...]).T


SCALAR = pl.BlockSpec(memory_space=pltpu.SMEM)
FULL = pl.BlockSpec(memory_space=pltpu.VMEM)


def call(kernel, outs, args, scratch=(), scalar=True, name=None):
    return pl.pallas_call(
        kernel,
        out_shape=[jax.ShapeDtypeStruct(s, t) for s, t in outs],
        in_specs=([SCALAR] if scalar else []) + [FULL] * (len(args) - bool(scalar)),
        out_specs=[FULL] * len(outs),
        scratch_shapes=list(scratch),
        name=name,
    )(*args)


def exchange(msg, domains):
    x = msg.reshape(domains, ROWS // 4, 4, msg.shape[1])
    x = lax.all_to_all(x, "dom", split_axis=0, concat_axis=0, tiled=True)
    return x.reshape(msg.shape)


def local(
    increments,
    w_in,
    w_node1,
    w_node2,
    w_out,
    grid_edges,
    mesh_edges,
    mesh_mask,
    send_rows,
    site_owner,
    site_nodes,
    site_obs,
):
    domains = lax.axis_size("dom")
    feat = lax.axis_index("feat").astype(I32).reshape(1)
    grid_rows, variables = increments.shape
    mesh_rows = mesh_edges.shape[0]
    inner = w_node2.shape[0]
    site_count = site_obs.shape[0]
    half = mesh_rows // 2
    rows = domains * ROWS
    send = send_rows[0]
    msg, ginc, target = call(
        encode_kernel,
        [((rows, variables), BF), ((mesh_rows, variables), BF), ((site_count, 1), I32)],
        (feat, increments, grid_edges, send, site_owner, site_nodes, site_obs),
        [
            pltpu.VMEM((mesh_rows, grid_rows), BF),
            pltpu.VMEM((rows, mesh_rows), BF),
            pltpu.VMEM((rows, 1), I32),
        ],
        name="encode",
    )
    m, w_cat, w_ho, w_io = call(
        prepare_kernel,
        [
            ((mesh_rows, half + rows), BF),
            ((2 * variables, inner), BF),
            ((inner, variables), BF),
            ((variables, variables), BF),
        ],
        (feat, mesh_edges, mesh_mask, w_in, w_node1, w_node2, w_out),
        [pltpu.VMEM(mesh_edges.shape, I32)],
        name="prepare",
    )
    got = exchange(msg, domains)
    part, node = call(
        mix_kernel,
        [((mesh_rows + 2 * LANES, variables), BF), ((LANES, LANES), I32)],
        (feat, got, ginc, m),
        name="mix",
    )
    other = lax.ppermute(part, "feat", SWAP)
    (sites,) = call(
        site_kernel, [((SLOTS * domains, mesh_rows), BF)], (node,), scalar=False, name="sites"
    )
    back, own_t, ext_t = call(
        node_kernel,
        [
            ((rows, variables), BF),
            ((variables // 2, mesh_rows), F32),
            ((variables, half), F32),
        ],
        (feat, part, other, ginc, m, sites, w_cat, w_ho, w_io),
        [pltpu.VMEM((mesh_rows, inner), F32)],
        name="node",
    )
    got_back = exchange(back, domains)
    g, r = call(
        scatter_kernel,
        [((mesh_rows, grid_rows), BF), ((rows, mesh_rows), BF)],
        (feat, grid_edges, send),
        [pltpu.VMEM((rows, 1), I32)],
        name="scatter",
    )
    keep, give, site_pred = call(
        return_kernel,
        [
            ((variables // 2, mesh_rows), F32),
            ((variables // 2, mesh_rows), BF),
            ((site_count, variables), BF),
        ],
        (feat, got_back, r, ext_t, own_t, target),
        [pltpu.VMEM((variables, mesh_rows), F32)],
        name="return",
    )
    take = lax.ppermute(give, "feat", SWAP)
    chunk = 1024
    degree = grid_edges.shape[1]

    def grid_body(keep_ref, got_ref, g_ref, out_ref):
        grid_kernel(keep_ref, got_ref, g_ref, out_ref, degree=degree)

    grad_grid = pl.pallas_call(
        grid_body,
        grid=(grid_rows // chunk,),
        out_shape=jax.ShapeDtypeStruct((grid_rows, variables // 2), F32),
        in_specs=[
            pl.BlockSpec((variables // 2, mesh_rows), lambda i: (0, 0)),
            pl.BlockSpec((variables // 2, mesh_rows), lambda i: (0, 0)),
            pl.BlockSpec((mesh_rows, chunk), lambda i: (0, i)),
        ],
        out_specs=pl.BlockSpec((chunk, variables // 2), lambda i: (i, 0)),
        name="grid",
    )(keep, take, g)
    return (grad_grid, site_pred)


def solution(mesh):
    return jax.shard_map(
        local,
        mesh=mesh,
        in_specs=(
            P("dom", None),
            P(),
            P(),
            P(),
            P(),
            P("dom", None),
            P("dom", None),
            P("dom", None),
            P("dom", None, None),
            P("dom", None),
            P("dom", None),
            P("dom", None),
        ),
        out_specs=(P("dom", "feat"), P("dom", None)),
        check_vma=False,
    )
```

```python
import jax
import jax.numpy as jnp
from jax import lax
from jax.experimental import pallas as pl
from jax.experimental.pallas import tpu as pltpu
from jax.sharding import PartitionSpec as P

BF = jnp.bfloat16
F32 = jnp.float32
I16 = jnp.int16
I32 = jnp.int32
LANES = 128
HALF_DEPTH = 8
SLOTS = 4
ROWS = HALF_DEPTH + SLOTS
SWAP = [(0, 1), (1, 0)]


def dot(a, b, ca=1, cb=0):
    return lax.dot_general(a, b, (((ca,), (cb,)), ((), ())), preferred_element_type=F32)


def iota(shape, axis):
    return lax.broadcasted_iota(I32, shape, axis)


def eq_bf16(a, b):
    return jnp.where(a == b, jnp.asarray(1, BF), jnp.asarray(0, BF))


def build_counts(dst, tiles, height, lane0=0, sub=16, unroll=4):
    cols = [[jnp.broadcast_to(r, (sub, LANES)).astype(I16) for r in rows] for rows in tiles]
    start = iota((sub, LANES), 0).astype(I16)

    def body(i, at):
        s = pl.multiple_of(i * sub, sub)
        for t, rows in enumerate(cols):
            acc = eq_bf16(rows[0], at)
            for r in rows[1:]:
                acc = acc + eq_bf16(r, at)
            dst[pl.ds(s, sub), lane0 + t * LANES : lane0 + (t + 1) * LANES] = acc
        return at + jnp.asarray(sub, I16)

    lax.fori_loop(0, height // sub, body, start, unroll=unroll)


def lane_tiles(rows, first=0, last=None):
    last = rows.shape[1] // LANES if last is None else last
    return [
        [rows[k : k + 1, t * LANES : (t + 1) * LANES] for k in range(rows.shape[0])]
        for t in range(first, last)
    ]


def block_of(shape):
    row = iota(shape, 1)
    peer = jnp.floor((row.astype(F32) + 0.5) * (1.0 / ROWS)).astype(I32)
    return peer, row - peer * ROWS


def place_rows(dst, slots):
    c = iota((1, slots * LANES), 1)
    build_counts(dst, lane_tiles((c & 127) * ROWS + HALF_DEPTH + (c >> 7)), dst.shape[0])


def take_rows(dst, slots):
    peer, within = block_of((1, dst.shape[1]))
    slot = within - HALF_DEPTH
    build_counts(dst, lane_tiles(jnp.where(slot >= 0, slot * LANES + peer, -1)), slots * LANES)


def send_index(feat, send, rows):
    peers = send.shape[1]
    picked = jnp.where(feat == 0, send[:HALF_DEPTH, :], send[HALF_DEPTH:, :])
    table = jnp.concatenate([picked >> 5, picked & 31], axis=0).astype(F32).astype(BF)
    peer, within = block_of((1, rows))
    spread = jnp.where(iota((peers, rows), 0) == peer, 1.0, 0.0).astype(BF)
    out = dot(table, spread)
    node = out[:HALF_DEPTH, :] * 32.0 + out[HALF_DEPTH:, :]
    hit = iota((HALF_DEPTH, rows), 0) == within
    index = jnp.sum(jnp.where(hit, node, 0.0), axis=0, keepdims=True)
    return jnp.where(within >= HALF_DEPTH, -1.0, index).astype(I32)


def encode_kernel(feat_ref, inc, edges, send, owner, nodes, obs, msg, ginc, target, g, r, c_s):
    feat = feat_ref[0]
    rows = msg.shape[0]
    build_counts(g, lane_tiles(edges[...]), inc.shape[0])
    build_counts(r, lane_tiles(send_index(feat, send[...], rows)), ginc.shape[1])
    place_rows(c_s, 3)
    sites = owner.shape[1]
    own = owner[...]
    member = jnp.where(iota((LANES, sites), 0) == own, 1.0, 0.0)
    member_b = member.astype(BF)
    upper = jnp.where(iota((sites, sites), 0) < iota((sites, sites), 1), 1.0, 0.0).astype(BF)
    rank = jnp.sum(dot(member_b, upper) * member, axis=0, keepdims=True)
    target[...] = own * ROWS + HALF_DEPTH + rank.astype(I32)
    slot0 = (2 * feat).astype(F32)
    obs_0 = dot(jnp.where(rank == slot0, member, 0.0).astype(BF), obs[...])
    obs_1 = dot(jnp.where(rank == slot0 + 1.0, member, 0.0).astype(BF), obs[...])
    n = nodes[...]
    high = ((n >> 5) + 1).astype(F32)
    low = (n & 31).astype(F32)
    lists = [jnp.where(rank == float(k), v, 0.0) for v in (high, low) for k in range(SLOTS)]
    lists.append(jnp.zeros((LANES - 2 * SLOTS * n.shape[0], sites), F32))
    listed = dot(member_b, jnp.concatenate(lists, axis=0).astype(BF), 1, 1)
    site_rows = dot(c_s[...], jnp.concatenate([obs_0, obs_1, listed], axis=0).astype(BF))
    mean = (dot(inc[...], g[...], 0, 0) * (1.0 / edges.shape[0])).astype(BF)
    ginc[...] = mean
    msg[...] = (dot(mean, r[...]).T + site_rows).astype(BF)


def prepare_kernel(
    feat_ref, edges, mask, w_in, w_node1, w_node2, w_out, m, w_cat, w_cat_t, w_ho, w_ho_t, w_io, w_io_t
):
    feat = feat_ref[0]
    rows = edges.shape[1]
    half = rows // 2
    e = edges[...]
    own_row = e - feat * half
    h = e - rows
    r = h & 15
    halo_row = half + (h >> 4) * ROWS + (r & 7)
    is_own = (e < rows) & (own_row >= 0) & (own_row < half)
    is_halo = (e >= rows) & ((r >> 3) == feat)
    at = jnp.where(is_own, own_row, jnp.where(is_halo, halo_row, -1))
    at = jnp.where(mask[...] > 0, at, -1)
    tiles = lane_tiles(at)
    for first in range(0, len(tiles), 4):
        build_counts(m, tiles[first : first + 4], m.shape[0], first * LANES)
    width = w_in.shape[1]
    variables = w_in.shape[0]
    wi = w_in[...]
    for k in range(2):
        w1 = w_node1[k * width : (k + 1) * width, :]
        w_cat[k * variables : (k + 1) * variables, :] = dot(wi, w1).astype(BF)
        w_cat_t[:, k * variables : (k + 1) * variables] = dot(w1, wi, 0, 1).astype(BF)
    w_ho[...] = dot(w_node2[...], w_out[...]).astype(BF)
    w_ho_t[...] = dot(w_out[...], w_node2[...], 0, 1).astype(BF)
    w_io[...] = dot(wi, w_out[...]).astype(BF)
    w_io_t[...] = dot(w_out[...], wi, 0, 1).astype(BF)


def mix_kernel(feat_ref, msg, ginc, m, part, node, c_s):
    feat = feat_ref[0]
    rows = ginc.shape[1]
    half = rows // 2
    take_rows(c_s, 3)
    got = msg[...]
    own = ginc[:, pl.ds(pl.multiple_of(feat * half, half), half)]
    part[:, :rows] = (dot(own, m[:half, :]) + dot(got, m[half:, :], 0, 0)).astype(BF)
    sites = dot(c_s[...], got).T
    part[:, rows:] = sites[:, : 2 * LANES].astype(BF)
    lists = sites[: 2 * node.shape[0], 2 * LANES :]
    node[...] = ((lists[: node.shape[0], :] - 1.0) * 32.0 + lists[node.shape[0] :, :]).astype(I32)


def site_kernel(node, s):
    degree = node.shape[0] // SLOTS
    tiles = [[node[k * degree + j : k * degree + j + 1, :] for j in range(degree)] for k in range(SLOTS)]
    build_counts(s, tiles, s.shape[0])


def node_kernel(
    feat_ref, part, other, ginc, m, s, w_cat, w_cat_t, w_ho, w_ho_t, w_io, w_io_t, msg, own, ext_own, slope_s, c_s
):
    feat = feat_ref[0]
    variables, rows = ginc.shape
    half = rows // 2
    place_rows(c_s, SLOTS)
    gi = ginc[...]
    agg = (part[:, :rows].astype(F32) + other[:, :rows].astype(F32)).astype(BF)
    pre = dot(w_cat_t[...], jnp.concatenate([gi, agg], axis=0))
    sig = 1.0 / (1.0 + jnp.exp(-pre))
    hidden = (pre * sig).astype(BF)
    slope_s[...] = sig * (1.0 + pre * (1.0 - sig))
    readout = (dot(w_ho_t[...], hidden) + dot(w_io_t[...], gi)).astype(BF)
    values = dot(readout, s[...])
    mine = part[:, rows:].astype(F32)
    theirs = other[:, rows:].astype(F32)
    first = jnp.where(feat == 0, mine, theirs)
    second = jnp.where(feat == 0, theirs, mine)
    diff = (values - jnp.concatenate([first, second], axis=1)).astype(BF)
    d = dot(diff, s[...], 1, 1).astype(BF)
    inner = (dot(w_ho[...], d) * slope_s[...]).astype(BF)
    n = variables // 2
    cols = pl.ds(pl.multiple_of(feat * n, n), n)
    both = dot(jnp.concatenate([w_cat[cols, :], w_cat[variables:, :]], axis=0), inner)
    own[...] = dot(w_io[cols, :], d) + both[:n, :]
    ext = dot(m[...], both[n:, :].T.astype(BF))
    ext_own[...] = ext[:half, :].T
    msg[...] = (ext[half:, :] + dot(c_s[...], values.T.astype(BF))).astype(BF)


def scatter_kernel(feat_ref, edges, send, g, r):
    build_counts(g, lane_tiles(edges[...]), g.shape[0])
    build_counts(r, lane_tiles(send_index(feat_ref[0], send[...], r.shape[1])), r.shape[0])


def return_kernel(feat_ref, msg, r, ext_own, own, target, keep, give, pred, part_s, p_s):
    feat = feat_ref[0]
    half = ext_own.shape[1]
    build_counts(p_s, lane_tiles(target[...]), msg.shape[0])
    back = msg[...].T
    part_s[...] = dot(back, r[...], 1, 1)
    at = pl.ds(pl.multiple_of(feat * half, half), half)
    part_s[:, at] = part_s[:, at] + ext_own[...]
    n = keep.shape[0]
    keep[...] = part_s[pl.ds(pl.multiple_of(feat * n, n), n), :] + own[...]
    give[...] = part_s[pl.ds(pl.multiple_of((1 - feat) * n, n), n), :].astype(BF)
    pred[...] = dot(back, p_s[...]).T.astype(BF)


def grid_kernel(keep, got, g, out, *, degree):
    lg = ((keep[...] + got[...].astype(F32)) * (1.0 / degree)).astype(BF)
    out[...] = dot(lg, g[...], 1, 1)


SCALAR = pl.BlockSpec(memory_space=pltpu.SMEM)
FULL = pl.BlockSpec(memory_space=pltpu.VMEM)


def vmem(x):
    return pltpu.with_memory_space_constraint(x, pltpu.VMEM)


def call(kernel, outs, args, scratch=(), scalar=True, name=None):
    return pl.pallas_call(
        kernel,
        out_shape=[
            pltpu.VMEM(s, t) if stay else jax.ShapeDtypeStruct(s, t) for s, t, stay in outs
        ],
        in_specs=([SCALAR] if scalar else []) + [FULL] * (len(args) - bool(scalar)),
        out_specs=[FULL] * len(outs),
        scratch_shapes=list(scratch),
        name=name,
    )(*args)


def exchange(msg, domains):
    x = msg.reshape(domains, ROWS // 4, 4, msg.shape[1])
    x = lax.all_to_all(x, "dom", split_axis=0, concat_axis=0, tiled=True)
    return x.reshape(msg.shape)


def local(
    increments,
    w_in,
    w_node1,
    w_node2,
    w_out,
    grid_edges,
    mesh_edges,
    mesh_mask,
    send_rows,
    site_owner,
    site_nodes,
    site_obs,
):
    domains = lax.axis_size("dom")
    feat = lax.axis_index("feat").astype(I32).reshape(1)
    grid_rows, variables = increments.shape
    mesh_rows = mesh_edges.shape[0]
    inner = w_node2.shape[0]
    site_count = site_obs.shape[0]
    half = mesh_rows // 2
    rows = domains * ROWS
    degree = grid_edges.shape[1]
    n = variables // 2
    msg, ginc, target = call(
        encode_kernel,
        [
            ((rows, variables), BF, False),
            ((variables, mesh_rows), BF, False),
            ((1, site_count), I32, False),
        ],
        (feat, increments, grid_edges.T, send_rows[0].T, site_owner.T, site_nodes.T, site_obs),
        [
            pltpu.VMEM((grid_rows, mesh_rows), BF),
            pltpu.VMEM((mesh_rows, rows), BF),
            pltpu.VMEM((rows, 3 * LANES), BF),
        ],
        name="encode",
    )
    m, *weights = call(
        prepare_kernel,
        [
            ((half + rows, mesh_rows), BF, False),
            ((2 * variables, inner), BF, False),
            ((inner, 2 * variables), BF, False),
            ((inner, variables), BF, False),
            ((variables, inner), BF, False),
            ((variables, variables), BF, False),
            ((variables, variables), BF, False),
        ],
        (feat, mesh_edges.T, mesh_mask.T, w_in, w_node1, w_node2, w_out),
        name="prepare",
    )
    got = exchange(msg, domains)
    part, node = call(
        mix_kernel,
        [
            ((variables, mesh_rows + 2 * LANES), BF, True),
            ((SLOTS * site_nodes.shape[1], LANES), I32, True),
        ],
        (feat, vmem(got), ginc, m),
        [pltpu.VMEM((3 * LANES, rows), BF)],
        name="mix",
    )
    other = lax.ppermute(part, "feat", SWAP)
    (sites,) = call(
        site_kernel, [((mesh_rows, SLOTS * domains), BF, True)], (vmem(node),), scalar=False, name="sites"
    )
    back, own, ext_own = call(
        node_kernel,
        [
            ((rows, variables), BF, False),
            ((n, mesh_rows), F32, False),
            ((variables, half), F32, False),
        ],
        (feat, vmem(part), vmem(other), ginc, m, vmem(sites), *weights),
        [pltpu.VMEM((inner, mesh_rows), F32), pltpu.VMEM((rows, SLOTS * LANES), BF)],
        name="node",
    )
    got_back = exchange(back, domains)
    g, r = call(
        scatter_kernel,
        [((grid_rows, mesh_rows), BF, False), ((mesh_rows, rows), BF, False)],
        (feat, grid_edges.T, send_rows[0].T),
        name="scatter",
    )
    keep, give, site_pred = call(
        return_kernel,
        [
            ((n, mesh_rows), F32, False),
            ((n, mesh_rows), BF, False),
            ((site_count, variables), BF, False),
        ],
        (feat, vmem(got_back), r, ext_own, own, target),
        [pltpu.VMEM((variables, mesh_rows), F32), pltpu.VMEM((rows, site_count), BF)],
        name="return",
    )
    take = lax.ppermute(give, "feat", SWAP)

    def grid_body(keep_ref, got_ref, g_ref, out_ref):
        grid_kernel(keep_ref, got_ref, g_ref, out_ref, degree=degree)

    (grad,) = call(
        grid_body,
        [((n, grid_rows), F32, False)],
        (keep, vmem(take), g),
        scalar=False,
        name="grid",
    )
    return (grad.T, site_pred)


def solution(mesh):
    return jax.shard_map(
        local,
        mesh=mesh,
        in_specs=(
            P("dom", None),
            P(),
            P(),
            P(),
            P(),
            P("dom", None),
            P("dom", None),
            P("dom", None),
            P("dom", None, None),
            P("dom", None),
            P("dom", None),
            P("dom", None),
        ),
        out_specs=(P("dom", "feat"), P("dom", None)),
        check_vma=False,
    )
```

```python
import jax
import jax.numpy as jnp
from jax import lax
from jax.experimental import pallas as pl
from jax.experimental.pallas import tpu as pltpu
from jax.sharding import PartitionSpec as P

BF = jnp.bfloat16
F32 = jnp.float32
I16 = jnp.int16
I32 = jnp.int32
LANES = 128
HALF_DEPTH = 8
SLOTS = 4
ROWS = HALF_DEPTH + SLOTS
SWAP = [(0, 1), (1, 0)]
CHUNK = 512


def dot(a, b, ca=1, cb=0):
    return lax.dot_general(a, b, (((ca,), (cb,)), ((), ())), preferred_element_type=F32)


def iota(shape, axis):
    return lax.broadcasted_iota(I32, shape, axis)


def eq_bf16(a, b):
    return jnp.where(a == b, jnp.asarray(1, BF), jnp.asarray(0, BF))


def build_counts(dst, tiles, height, lane0=0, row0=0, sub=16, unroll=4):
    cols = [[jnp.broadcast_to(r, (sub, LANES)).astype(I16) for r in rows] for rows in tiles]
    start = (iota((sub, LANES), 0) + row0).astype(I16)

    def body(i, at):
        s = pl.multiple_of(row0 + i * sub, sub)
        for t, rows in enumerate(cols):
            acc = eq_bf16(rows[0], at)
            for r in rows[1:]:
                acc = acc + eq_bf16(r, at)
            dst[pl.ds(s, sub), lane0 + t * LANES : lane0 + (t + 1) * LANES] = acc
        return at + jnp.asarray(sub, I16)

    lax.fori_loop(0, height // sub, body, start, unroll=unroll)


def row_copies(src, dst, sems, starts, size, targets=None):
    targets = starts if targets is None else targets
    return [
        pltpu.make_async_copy(src.at[pl.ds(a, size), :], dst.at[pl.ds(b, size), :], sems.at[k])
        for k, (a, b) in enumerate(zip(starts, targets))
    ]


def chunks(total):
    return range(0, total, CHUNK)


def lane_tiles(rows, first=0, last=None):
    last = rows.shape[1] // LANES if last is None else last
    return [
        [rows[k : k + 1, t * LANES : (t + 1) * LANES] for k in range(rows.shape[0])]
        for t in range(first, last)
    ]


def block_of(shape):
    row = iota(shape, 1)
    peer = jnp.floor((row.astype(F32) + 0.5) * (1.0 / ROWS)).astype(I32)
    return peer, row - peer * ROWS


def place_rows(dst, slots):
    c = iota((1, slots * LANES), 1)
    build_counts(dst, lane_tiles((c & 127) * ROWS + HALF_DEPTH + (c >> 7)), dst.shape[0])


def take_rows(dst, slots):
    peer, within = block_of((1, dst.shape[1]))
    slot = within - HALF_DEPTH
    build_counts(dst, lane_tiles(jnp.where(slot >= 0, slot * LANES + peer, -1)), slots * LANES)


def send_index(picked, rows):
    peers = picked.shape[1]
    table = jnp.concatenate([picked >> 5, picked & 31], axis=0).astype(F32).astype(BF)
    peer, within = block_of((1, rows))
    spread = jnp.where(iota((peers, rows), 0) == peer, 1.0, 0.0).astype(BF)
    out = dot(table, spread)
    node = out[:HALF_DEPTH, :] * 32.0 + out[HALF_DEPTH:, :]
    hit = iota((HALF_DEPTH, rows), 0) == within
    index = jnp.sum(jnp.where(hit, node, 0.0), axis=0, keepdims=True)
    return jnp.where(within >= HALF_DEPTH, -1.0, index).astype(I32)


def encode_kernel(
    feat_ref, inc_h, edges, send, owner, nodes, obs, msg, ginc, target, g, r, c_s, inc, sem
):
    feat = feat_ref[0]
    rows = msg.shape[0]
    load = pltpu.make_async_copy(inc_h, inc, sem)
    load.start()
    build_counts(g, lane_tiles(edges[...]), inc.shape[0])
    picked = jnp.where(feat == 0, send[:HALF_DEPTH, :], send[HALF_DEPTH:, :])
    build_counts(r, lane_tiles(send_index(picked, rows)), ginc.shape[1])
    place_rows(c_s, 3)
    sites = owner.shape[1]
    own = owner[...]
    member = jnp.where(iota((LANES, sites), 0) == own, 1.0, 0.0)
    member_b = member.astype(BF)
    upper = jnp.where(iota((sites, sites), 0) < iota((sites, sites), 1), 1.0, 0.0).astype(BF)
    rank = jnp.sum(dot(member_b, upper) * member, axis=0, keepdims=True)
    target[...] = own * ROWS + HALF_DEPTH + rank.astype(I32)
    slot0 = (2 * feat).astype(F32)
    obs_0 = dot(jnp.where(rank == slot0, member, 0.0).astype(BF), obs[...])
    obs_1 = dot(jnp.where(rank == slot0 + 1.0, member, 0.0).astype(BF), obs[...])
    n = nodes[...]
    high = ((n >> 5) + 1).astype(F32)
    low = (n & 31).astype(F32)
    lists = [jnp.where(rank == float(k), v, 0.0) for v in (high, low) for k in range(SLOTS)]
    lists.append(jnp.zeros((LANES - 2 * SLOTS * n.shape[0], sites), F32))
    listed = dot(member_b, jnp.concatenate(lists, axis=0).astype(BF), 1, 1)
    site_rows = dot(c_s[...], jnp.concatenate([obs_0, obs_1, listed], axis=0).astype(BF))
    load.wait()
    mean = (dot(inc[...], g[...], 0, 0) * (1.0 / edges.shape[0])).astype(BF)
    ginc[...] = mean
    msg[...] = (dot(mean, r[...]).T + site_rows).astype(BF)


def prepare_kernel(
    edges, mask, w_in, w_node1, w_node2, w_out, m_h, w_cat, w_cat_t, w_ho, w_ho_t, w_io, w_io_t, m, sems
):
    rows = edges.shape[1]
    width = w_in.shape[1]
    variables = w_in.shape[0]
    wi = w_in[...]
    for k in range(2):
        w1 = w_node1[k * width : (k + 1) * width, :]
        w_cat[k * variables : (k + 1) * variables, :] = dot(wi, w1).astype(BF)
        w_cat_t[:, k * variables : (k + 1) * variables] = dot(w1, wi, 0, 1).astype(BF)
    w_ho[...] = dot(w_node2[...], w_out[...]).astype(BF)
    w_ho_t[...] = dot(w_out[...], w_node2[...], 0, 1).astype(BF)
    w_io[...] = dot(wi, w_out[...]).astype(BF)
    w_io_t[...] = dot(w_out[...], wi, 0, 1).astype(BF)
    e = edges[...]
    h = e - rows
    r = h & 15
    halo_row = rows + (r >> 3) * ((m.shape[0] - rows) // 2) + (h >> 4) * ROWS + (r & 7)
    at = jnp.where(mask[...] > 0, jnp.where(e < rows, e, halo_row), -1)
    tiles = lane_tiles(at)
    copies = row_copies(m, m_h, sems, chunks(m.shape[0]), CHUNK)
    for row0, copy in zip(chunks(m.shape[0]), copies):
        for first in range(0, len(tiles), 4):
            build_counts(m, tiles[first : first + 4], CHUNK, first * LANES, row0)
        copy.start()
    for copy in copies:
        copy.wait()


def mix_kernel(feat_ref, msg, ginc, m_h, part, node, c_s, m, sems):
    feat = feat_ref[0]
    rows = ginc.shape[1]
    half = rows // 2
    halo = rows + feat * msg.shape[0]
    starts = [feat * half] + [halo + k for k in chunks(msg.shape[0])]
    copies = row_copies(m_h, m, sems, starts, CHUNK, chunks(m.shape[0]))
    for copy in copies:
        copy.start()
    take_rows(c_s, 3)
    got = msg[...]
    sites = dot(c_s[...], got).T
    part[:, rows:] = sites[:, : 2 * LANES].astype(BF)
    lists = sites[: 2 * node.shape[0], 2 * LANES :]
    node[...] = ((lists[: node.shape[0], :] - 1.0) * 32.0 + lists[node.shape[0] :, :]).astype(I32)
    copies[0].wait()
    acc = dot(ginc[:, pl.ds(pl.multiple_of(feat * half, half), half)], m[:half, :])
    for k, copy in zip(chunks(msg.shape[0]), copies[1:]):
        copy.wait()
        acc = acc + dot(msg[k : k + CHUNK, :], m[half + k : half + k + CHUNK, :], 0, 0)
    part[:, :rows] = acc.astype(BF)


def site_kernel(node, s):
    degree = node.shape[0] // SLOTS
    tiles = [[node[k * degree + j : k * degree + j + 1, :] for j in range(degree)] for k in range(SLOTS)]
    build_counts(s, tiles, s.shape[0])


def node_kernel(
    feat_ref, part, other, ginc, m_h, s, w_cat, w_cat_t, w_ho, w_ho_t, w_io, w_io_t, msg, own, slope_s, c_s, m, sems
):
    feat = feat_ref[0]
    variables, rows = ginc.shape
    copies = row_copies(m_h, m, sems, chunks(m.shape[0]), CHUNK)
    for copy in copies:
        copy.start()
    place_rows(c_s, SLOTS)
    gi = ginc[...]
    agg = (part[:, :rows].astype(F32) + other[:, :rows].astype(F32)).astype(BF)
    pre = dot(w_cat_t[...], jnp.concatenate([gi, agg], axis=0))
    sig = 1.0 / (1.0 + jnp.exp(-pre))
    hidden = (pre * sig).astype(BF)
    slope_s[...] = sig * (1.0 + pre * (1.0 - sig))
    readout = (dot(w_ho_t[...], hidden) + dot(w_io_t[...], gi)).astype(BF)
    values = dot(readout, s[...])
    mine = part[:, rows:].astype(F32)
    theirs = other[:, rows:].astype(F32)
    first = jnp.where(feat == 0, mine, theirs)
    second = jnp.where(feat == 0, theirs, mine)
    diff = (values - jnp.concatenate([first, second], axis=1)).astype(BF)
    d = dot(diff, s[...], 1, 1).astype(BF)
    inner = (dot(w_ho[...], d) * slope_s[...]).astype(BF)
    n = variables // 2
    cols = pl.ds(pl.multiple_of(feat * n, n), n)
    agg_cols = pl.ds(pl.multiple_of(variables + feat * n, n), n)
    both = dot(jnp.concatenate([w_cat[cols, :], w_cat[agg_cols, :]], axis=0), inner)
    agg_grad = both[n:, :].T.astype(BF)
    placed = dot(c_s[...], values.T.astype(BF))
    for copy in copies:
        copy.wait()
    own[...] = dot(w_io[cols, :], d) + both[:n, :] + dot(m[:rows, :], agg_grad).T
    count = msg.shape[0]
    low = dot(m[rows : rows + count, :], agg_grad)
    high = dot(m[rows + count :, :], agg_grad)
    msg[...] = (jnp.concatenate([low, high], axis=1) + placed).astype(BF)


def scatter_kernel(edges, g_h, g, sems):
    tiles = lane_tiles(edges[...])
    copies = row_copies(g, g_h, sems, chunks(g.shape[0]), CHUNK)
    for row0, copy in zip(chunks(g.shape[0]), copies):
        build_counts(g, tiles, CHUNK, 0, row0)
        copy.start()
    for copy in copies:
        copy.wait()


def finish_kernel(msg, send, own, target, g_h, out_h, pred, r, p_s, g, out, in_sems, out_sems, *, degree):
    copies = row_copies(g_h, g, in_sems, chunks(g.shape[0]), CHUNK)
    for copy in copies:
        copy.start()
    count = msg.shape[0]
    for k in range(2):
        picked = send[k * HALF_DEPTH : (k + 1) * HALF_DEPTH, :]
        build_counts(r, lane_tiles(send_index(picked, count)), r.shape[0], k * count)
    build_counts(p_s, lane_tiles(target[...]), count)
    back = msg[...].T
    n = own.shape[0]
    pred[...] = dot(back, p_s[...]).T.astype(BF)
    grad = own[...] + dot(back[:n, :], r[:, :count], 1, 1) + dot(back[n:, :], r[:, count:], 1, 1)
    grad = (grad * (1.0 / degree)).astype(BF)
    stores = []
    for k, (a, copy) in enumerate(zip(chunks(g.shape[0]), copies)):
        copy.wait()
        out[:, a : a + CHUNK] = dot(grad, g[a : a + CHUNK, :], 1, 1)
        stores.append(
            pltpu.make_async_copy(
                out.at[:, pl.ds(a, CHUNK)], out_h.at[:, pl.ds(a, CHUNK)], out_sems.at[k]
            )
        )
        stores[-1].start()
    for store in stores:
        store.wait()


SCALAR = pl.BlockSpec(memory_space=pltpu.SMEM)
FULL = pl.BlockSpec(memory_space=pltpu.VMEM)
HBM = pl.BlockSpec(memory_space=pl.ANY)
STAY, LEAVE, COPY = "stay", "leave", "copy"


def vmem(x):
    return pltpu.with_memory_space_constraint(x, pltpu.VMEM)


def dma(n):
    return pltpu.SemaphoreType.DMA((n,))


def call(kernel, outs, args, scratch=(), scalar=True, far=(), name=None):
    return pl.pallas_call(
        kernel,
        out_shape=[
            pltpu.VMEM(s, t) if where == STAY else jax.ShapeDtypeStruct(s, t) for s, t, where in outs
        ],
        in_specs=[
            SCALAR if scalar and k == 0 else HBM if k in far else FULL for k in range(len(args))
        ],
        out_specs=[HBM if where == COPY else FULL for _, _, where in outs],
        scratch_shapes=list(scratch),
        name=name,
    )(*args)


def exchange(msg, domains):
    x = msg.reshape(domains, ROWS // 4, 4, msg.shape[1])
    x = lax.all_to_all(x, "dom", split_axis=0, concat_axis=0, tiled=True)
    return x.reshape(msg.shape)


def local(
    increments,
    w_in,
    w_node1,
    w_node2,
    w_out,
    grid_edges,
    mesh_edges,
    mesh_mask,
    send_rows,
    site_owner,
    site_nodes,
    site_obs,
):
    domains = lax.axis_size("dom")
    feat = lax.axis_index("feat").astype(I32).reshape(1)
    grid_rows, variables = increments.shape
    mesh_rows = mesh_edges.shape[0]
    inner = w_node2.shape[0]
    site_count = site_obs.shape[0]
    rows = domains * ROWS
    degree = grid_edges.shape[1]
    n = variables // 2
    neighbours = mesh_rows + 2 * rows
    grid_t = grid_edges.T
    send_t = send_rows[0].T
    msg, ginc, target = call(
        encode_kernel,
        [
            ((rows, variables), BF, LEAVE),
            ((variables, mesh_rows), BF, LEAVE),
            ((1, site_count), I32, LEAVE),
        ],
        (feat, increments, grid_t, send_t, site_owner.T, site_nodes.T, site_obs),
        [
            pltpu.VMEM((grid_rows, mesh_rows), BF),
            pltpu.VMEM((mesh_rows, rows), BF),
            pltpu.VMEM((rows, 3 * LANES), BF),
            pltpu.VMEM((grid_rows, variables), BF),
            pltpu.SemaphoreType.DMA,
        ],
        far=(1,),
        name="encode",
    )
    m, *weights = call(
        prepare_kernel,
        [
            ((neighbours, mesh_rows), BF, COPY),
            ((2 * variables, inner), BF, LEAVE),
            ((inner, 2 * variables), BF, LEAVE),
            ((inner, variables), BF, LEAVE),
            ((variables, inner), BF, LEAVE),
            ((variables, variables), BF, LEAVE),
            ((variables, variables), BF, LEAVE),
        ],
        (mesh_edges.T, mesh_mask.T, w_in, w_node1, w_node2, w_out),
        [pltpu.VMEM((neighbours, mesh_rows), BF), dma(neighbours // CHUNK)],
        scalar=False,
        name="prepare",
    )
    got = exchange(msg, domains)
    part, node = call(
        mix_kernel,
        [
            ((variables, mesh_rows + 2 * LANES), BF, STAY),
            ((SLOTS * site_nodes.shape[1], LANES), I32, STAY),
        ],
        (feat, vmem(got), ginc, m),
        [
            pltpu.VMEM((3 * LANES, rows), BF),
            pltpu.VMEM((mesh_rows // 2 + rows, mesh_rows), BF),
            dma((mesh_rows // 2 + rows) // CHUNK),
        ],
        far=(3,),
        name="mix",
    )
    other = lax.ppermute(part, "feat", SWAP)
    (sites,) = call(
        site_kernel,
        [((mesh_rows, SLOTS * domains), BF, STAY)],
        (vmem(node),),
        scalar=False,
        name="sites",
    )
    back, own = call(
        node_kernel,
        [((rows, variables), BF, LEAVE), ((n, mesh_rows), F32, LEAVE)],
        (feat, vmem(part), vmem(other), ginc, m, vmem(sites), *weights),
        [
            pltpu.VMEM((inner, mesh_rows), F32),
            pltpu.VMEM((rows, SLOTS * LANES), BF),
            pltpu.VMEM((neighbours, mesh_rows), BF),
            dma(neighbours // CHUNK),
        ],
        far=(4,),
        name="node",
    )
    got_back = exchange(back, domains)
    (g,) = call(
        scatter_kernel,
        [((grid_rows, mesh_rows), BF, COPY)],
        (grid_t,),
        [pltpu.VMEM((grid_rows, mesh_rows), BF), dma(grid_rows // CHUNK)],
        scalar=False,
        name="scatter",
    )

    def finish(*refs):
        finish_kernel(*refs, degree=degree)

    grad, site_pred = call(
        finish,
        [((n, grid_rows), F32, COPY), ((site_count, variables), BF, LEAVE)],
        (vmem(got_back), send_t, own, target, g),
        [
            pltpu.VMEM((mesh_rows, 2 * rows), BF),
            pltpu.VMEM((rows, site_count), BF),
            pltpu.VMEM((grid_rows, mesh_rows), BF),
            pltpu.VMEM((n, grid_rows), F32),
            dma(grid_rows // CHUNK),
            dma(grid_rows // CHUNK),
        ],
        scalar=False,
        far=(4,),
        name="finish",
    )
    return (grad.T, site_pred)


def solution(mesh):
    return jax.shard_map(
        local,
        mesh=mesh,
        in_specs=(
            P("dom", None),
            P(),
            P(),
            P(),
            P(),
            P("dom", None),
            P("dom", None),
            P("dom", None),
            P("dom", None, None),
            P("dom", None),
            P("dom", None),
            P("dom", None),
        ),
        out_specs=(P("dom", "feat"), P("dom", None)),
        check_vma=False,
    )
```

```python
import jax
import jax.numpy as jnp
from jax import lax
from jax.experimental import pallas as pl
from jax.experimental.pallas import tpu as pltpu
from jax.sharding import PartitionSpec as P

BF = jnp.bfloat16
F32 = jnp.float32
I16 = jnp.int16
I32 = jnp.int32
LANES = 128
HALF_DEPTH = 8
SLOTS = 4
ROWS = HALF_DEPTH + SLOTS
SWAP = [(0, 1), (1, 0)]
CHUNK = 512


def dot(a, b, ca=1, cb=0):
    return lax.dot_general(a, b, (((ca,), (cb,)), ((), ())), preferred_element_type=F32)


def iota(shape, axis):
    return lax.broadcasted_iota(I32, shape, axis)


def eq_bf16(a, b):
    return jnp.where(a == b, jnp.asarray(1, BF), jnp.asarray(0, BF))


def build_counts(dst, tiles, height, lane0=0, row0=0, sub=16, unroll=4):
    cols = [[jnp.broadcast_to(r, (sub, LANES)).astype(I16) for r in rows] for rows in tiles]
    start = (iota((sub, LANES), 0) + row0).astype(I16)

    def body(i, at):
        s = pl.multiple_of(row0 + i * sub, sub)
        for t, rows in enumerate(cols):
            acc = eq_bf16(rows[0], at)
            for r in rows[1:]:
                acc = acc + eq_bf16(r, at)
            dst[pl.ds(s, sub), lane0 + t * LANES : lane0 + (t + 1) * LANES] = acc
        return at + jnp.asarray(sub, I16)

    lax.fori_loop(0, height // sub, body, start, unroll=unroll)


def build_rows(dst, index, rows, degree, block=128, unroll=2, after=None):
    start = iota((block, LANES), 1).astype(I16)
    for n, s in enumerate(range(0, rows, block)):
        cols = [
            jnp.broadcast_to(index[s : s + block, k : k + 1], (block, LANES)).astype(I16)
            for k in range(degree)
        ]

        def body(w, at, s=s, cols=cols):
            acc = eq_bf16(cols[0], at)
            for c in cols[1:]:
                acc = acc + eq_bf16(c, at)
            dst[s : s + block, pl.ds(pl.multiple_of(w * LANES, LANES), LANES)] = acc
            return at + jnp.asarray(LANES, I16)

        lax.fori_loop(0, dst.shape[1] // LANES, body, start, unroll=unroll)
        if after is not None:
            after(n)


def row_copies(src, dst, sems, starts, size, targets=None):
    targets = starts if targets is None else targets
    return [
        pltpu.make_async_copy(src.at[pl.ds(a, size), :], dst.at[pl.ds(b, size), :], sems.at[k])
        for k, (a, b) in enumerate(zip(starts, targets))
    ]


def chunks(total):
    return range(0, total, CHUNK)


def lane_tiles(rows, first=0, last=None):
    last = rows.shape[1] // LANES if last is None else last
    return [
        [rows[k : k + 1, t * LANES : (t + 1) * LANES] for k in range(rows.shape[0])]
        for t in range(first, last)
    ]


def peer_rows(k):
    return pl.ds(k, LANES, stride=ROWS)


def encode_kernel(
    feat_ref, inc_h, edges, send, owner, nodes, obs, msg, ginc, target, g, r, wide, inc, sem
):
    feat = feat_ref[0]
    load = pltpu.make_async_copy(inc_h, inc, sem)
    load.start()
    build_counts(g, lane_tiles(edges[...]), inc.shape[0])
    picked = jnp.where(feat == 0, send[:HALF_DEPTH, :], send[HALF_DEPTH:, :])
    build_counts(r, [[picked[k : k + 1, :]] for k in range(HALF_DEPTH)], r.shape[0])
    sites = owner.shape[1]
    own = owner[...]
    member = jnp.where(iota((LANES, sites), 0) == own, 1.0, 0.0)
    member_b = member.astype(BF)
    upper = jnp.where(iota((sites, sites), 0) < iota((sites, sites), 1), 1.0, 0.0).astype(BF)
    rank = jnp.sum(dot(member_b, upper) * member, axis=0, keepdims=True)
    target[...] = rank.astype(I32) * LANES + own
    for k in range(2):
        slot = (2 * feat + k).astype(F32)
        wide[peer_rows(HALF_DEPTH + k), :] = dot(
            jnp.where(rank == slot, member, 0.0).astype(BF), obs[...]
        )
    n = nodes[...]
    high = ((n >> 5) + 1).astype(F32)
    low = (n & 31).astype(F32)
    lists = [jnp.where(rank == float(k), v, 0.0) for v in (high, low) for k in range(SLOTS)]
    lists.append(jnp.zeros((LANES - 2 * SLOTS * n.shape[0], sites), F32))
    listed = jnp.concatenate(lists, axis=0).astype(BF)
    wide[peer_rows(HALF_DEPTH + 2), :] = dot(member_b, listed, 1, 1)
    wide[peer_rows(HALF_DEPTH + 3), :] = jnp.zeros((LANES, LANES), F32)
    load.wait()
    mean = (dot(inc[...], g[...], 0, 0) * (1.0 / edges.shape[0])).astype(BF)
    ginc[...] = mean
    out = dot(mean, r[...])
    for k in range(HALF_DEPTH):
        wide[peer_rows(k), :] = out[:, k * LANES : (k + 1) * LANES].T
    msg[...] = wide[...].astype(BF)


def prepare_kernel(
    edges, mask, w_in, w_node1, w_node2, w_out, m_h, w_cat, w_cat_t, w_ho, w_ho_t, w_io, w_io_t, m, sems
):
    rows = edges.shape[1]
    width = w_in.shape[1]
    variables = w_in.shape[0]
    wi = w_in[...]
    for k in range(2):
        w1 = w_node1[k * width : (k + 1) * width, :]
        w_cat[k * variables : (k + 1) * variables, :] = dot(wi, w1).astype(BF)
        w_cat_t[:, k * variables : (k + 1) * variables] = dot(w1, wi, 0, 1).astype(BF)
    w_ho[...] = dot(w_node2[...], w_out[...]).astype(BF)
    w_ho_t[...] = dot(w_out[...], w_node2[...], 0, 1).astype(BF)
    w_io[...] = dot(wi, w_out[...]).astype(BF)
    w_io_t[...] = dot(w_out[...], wi, 0, 1).astype(BF)
    e = edges[...]
    h = e - rows
    r = h & 15
    at = jnp.where(mask[...] > 0, jnp.where(e < rows, e, rows + r * LANES + (h >> 4)), -1)
    tiles = lane_tiles(at)
    copies = row_copies(m, m_h, sems, chunks(m.shape[0]), CHUNK)
    for row0, copy in zip(chunks(m.shape[0]), copies):
        for first in range(0, len(tiles), 4):
            build_counts(m, tiles[first : first + 4], CHUNK, first * LANES, row0)
        copy.start()
    for copy in copies:
        copy.wait()


def mix_kernel(feat_ref, msg, ginc, m_h, part, node, wide, m, sems):
    feat = feat_ref[0]
    rows = ginc.shape[1]
    half = rows // 2
    count = HALF_DEPTH * LANES
    halo = rows + feat * count
    starts = [feat * half] + [halo + k for k in range(0, count, CHUNK)]
    copies = row_copies(m_h, m, sems, starts, CHUNK, chunks(m.shape[0]))
    for copy in copies:
        copy.start()
    wide[...] = msg[...].astype(F32)
    for k in range(2):
        part[:, rows + k * LANES : rows + (k + 1) * LANES] = (
            wide[peer_rows(HALF_DEPTH + k), :].T.astype(BF)
        )
    lists = wide[peer_rows(HALF_DEPTH + 2), :].T
    n = node.shape[0]
    node[...] = ((lists[:n, :] - 1.0) * 32.0 + lists[n : 2 * n, :]).astype(I32)
    got = jnp.concatenate([wide[peer_rows(k), :].T for k in range(HALF_DEPTH)], axis=1).astype(BF)
    copies[0].wait()
    acc = dot(ginc[:, pl.ds(pl.multiple_of(feat * half, half), half)], m[:half, :])
    for k, copy in zip(range(0, count, CHUNK), copies[1:]):
        copy.wait()
        acc = acc + dot(got[:, k : k + CHUNK], m[half + k : half + k + CHUNK, :])
    part[:, :rows] = acc.astype(BF)


def site_kernel(node, s):
    degree = node.shape[0] // SLOTS
    tiles = [[node[k * degree + j : k * degree + j + 1, :] for j in range(degree)] for k in range(SLOTS)]
    build_counts(s, tiles, s.shape[0])


def node_kernel(
    feat_ref, part, other, ginc, m_h, s, w_cat, w_cat_t, w_ho, w_ho_t, w_io, w_io_t, msg, own, slope_s, wide, m, sems
):
    feat = feat_ref[0]
    variables, rows = ginc.shape
    copies = row_copies(m_h, m, sems, chunks(m.shape[0]), CHUNK)
    for copy in copies:
        copy.start()
    gi = ginc[...]
    agg = (part[:, :rows].astype(F32) + other[:, :rows].astype(F32)).astype(BF)
    pre = dot(w_cat_t[...], jnp.concatenate([gi, agg], axis=0))
    sig = 1.0 / (1.0 + jnp.exp(-pre))
    hidden = (pre * sig).astype(BF)
    slope_s[...] = sig * (1.0 + pre * (1.0 - sig))
    readout = (dot(w_ho_t[...], hidden) + dot(w_io_t[...], gi)).astype(BF)
    values = dot(readout, s[...])
    mine = part[:, rows:].astype(F32)
    theirs = other[:, rows:].astype(F32)
    first = jnp.where(feat == 0, mine, theirs)
    second = jnp.where(feat == 0, theirs, mine)
    diff = (values - jnp.concatenate([first, second], axis=1)).astype(BF)
    d = dot(diff, s[...], 1, 1).astype(BF)
    inner = (dot(w_ho[...], d) * slope_s[...]).astype(BF)
    n = variables // 2
    cols = pl.ds(pl.multiple_of(feat * n, n), n)
    agg_cols = pl.ds(pl.multiple_of(variables + feat * n, n), n)
    both = dot(jnp.concatenate([w_cat[cols, :], w_cat[agg_cols, :]], axis=0), inner)
    agg_grad = both[n:, :].T.astype(BF)
    site_rows = values.T
    for k in range(SLOTS):
        wide[peer_rows(HALF_DEPTH + k), :] = site_rows[k * LANES : (k + 1) * LANES, :]
    for copy in copies:
        copy.wait()
    own[...] = dot(w_io[cols, :], d) + both[:n, :] + dot(m[:rows, :], agg_grad).T
    count = HALF_DEPTH * LANES
    low = dot(m[rows : rows + count, :], agg_grad)
    high = dot(m[rows + count :, :], agg_grad)
    halo = jnp.concatenate([low, high], axis=1)
    for k in range(HALF_DEPTH):
        wide[peer_rows(k), :] = halo[k * LANES : (k + 1) * LANES, :]
    msg[...] = wide[...].astype(BF)


def scatter_kernel(edges, target, g_h, target_col, g, sems):
    e = edges[...]
    columns = jnp.concatenate([e, e], axis=0).T
    block = g.shape[0] // sems.shape[0]
    copies = row_copies(g, g_h, sems, range(0, g.shape[0], block), block)
    build_rows(g, columns, g.shape[0], e.shape[0], block, after=lambda n: copies[n].start())
    target_col[...] = jnp.broadcast_to(target[...], (8, target.shape[1])).T[:, :1]
    for copy in copies:
        copy.wait()


def finish_kernel(msg, send, own, target, g_h, out_h, pred, wide, r, g, out, in_sems, out_sems, *, degree):
    width = g.shape[1] // in_sems.shape[0]
    spans = [pl.ds(k * width, width) for k in range(in_sems.shape[0])]
    loads = [
        pltpu.make_async_copy(g_h.at[:, at], g.at[:, at], in_sems.at[k]) for k, at in enumerate(spans)
    ]
    stores = [
        pltpu.make_async_copy(out.at[:, at], out_h.at[:, at], out_sems.at[k])
        for k, at in enumerate(spans)
    ]
    for load in loads:
        load.start()
    depth = send.shape[0]
    build_counts(r, [[send[k : k + 1, :]] for k in range(depth)], r.shape[0], unroll=2)
    wide[...] = msg[...].astype(F32)
    back = jnp.concatenate([wide[peer_rows(k), :] for k in range(HALF_DEPTH)], axis=0).astype(BF)
    count = back.shape[0]
    n = own.shape[0]
    low = dot(r[:, :count], back).T
    high = dot(r[:, count:], back).T
    grad = ((own[...] + low[:n, :] + high[n:, :]) * (1.0 / degree)).astype(BF)
    slots = [wide[peer_rows(HALF_DEPTH + k), :] for k in range(SLOTS)]
    pick = jnp.where(target[...] == iota((target.shape[0], SLOTS * LANES), 1), 1.0, 0.0).astype(BF)
    pred[...] = dot(pick, jnp.concatenate(slots, axis=0).astype(BF)).astype(BF)
    for at, load, store in zip(spans, loads, stores):
        load.wait()
        out[:, at] = dot(grad, g[:, at])
        store.start()
    for store in stores:
        store.wait()


SCALAR = pl.BlockSpec(memory_space=pltpu.SMEM)
FULL = pl.BlockSpec(memory_space=pltpu.VMEM)
HBM = pl.BlockSpec(memory_space=pl.ANY)
STAY, LEAVE, COPY = "stay", "leave", "copy"


def vmem(x):
    return pltpu.with_memory_space_constraint(x, pltpu.VMEM)


def dma(n):
    return pltpu.SemaphoreType.DMA((n,))


def call(kernel, outs, args, scratch=(), scalar=True, far=(), name=None):
    return pl.pallas_call(
        kernel,
        out_shape=[
            pltpu.VMEM(s, t) if where == STAY else jax.ShapeDtypeStruct(s, t) for s, t, where in outs
        ],
        in_specs=[
            SCALAR if scalar and k == 0 else HBM if k in far else FULL for k in range(len(args))
        ],
        out_specs=[HBM if where == COPY else FULL for _, _, where in outs],
        scratch_shapes=list(scratch),
        name=name,
    )(*args)


def exchange(msg, domains):
    x = msg.reshape(domains, ROWS // 4, 4, msg.shape[1])
    x = lax.all_to_all(x, "dom", split_axis=0, concat_axis=0, tiled=True)
    return x.reshape(msg.shape)


def local(
    increments,
    w_in,
    w_node1,
    w_node2,
    w_out,
    grid_edges,
    mesh_edges,
    mesh_mask,
    send_rows,
    site_owner,
    site_nodes,
    site_obs,
):
    domains = lax.axis_size("dom")
    feat = lax.axis_index("feat").astype(I32).reshape(1)
    grid_rows, variables = increments.shape
    mesh_rows = mesh_edges.shape[0]
    inner = w_node2.shape[0]
    site_count = site_obs.shape[0]
    rows = domains * ROWS
    degree = grid_edges.shape[1]
    n = variables // 2
    neighbours = mesh_rows + 2 * HALF_DEPTH * domains
    wide = pltpu.VMEM((rows, variables), F32)
    grid_t = grid_edges.T
    send_t = send_rows[0].T
    msg, ginc, target = call(
        encode_kernel,
        [
            ((rows, variables), BF, LEAVE),
            ((variables, mesh_rows), BF, STAY),
            ((1, site_count), I32, LEAVE),
        ],
        (feat, increments, grid_t, send_t, site_owner.T, site_nodes.T, site_obs),
        [
            pltpu.VMEM((grid_rows, mesh_rows), BF),
            pltpu.VMEM((mesh_rows, HALF_DEPTH * domains), BF),
            wide,
            pltpu.VMEM((grid_rows, variables), BF),
            pltpu.SemaphoreType.DMA,
        ],
        far=(1,),
        name="encode",
    )
    m, *weights = call(
        prepare_kernel,
        [
            ((neighbours, mesh_rows), BF, COPY),
            ((2 * variables, inner), BF, LEAVE),
            ((inner, 2 * variables), BF, LEAVE),
            ((inner, variables), BF, LEAVE),
            ((variables, inner), BF, LEAVE),
            ((variables, variables), BF, LEAVE),
            ((variables, variables), BF, LEAVE),
        ],
        (mesh_edges.T, mesh_mask.T, w_in, w_node1, w_node2, w_out),
        [pltpu.VMEM((neighbours, mesh_rows), BF), dma(neighbours // CHUNK)],
        scalar=False,
        name="prepare",
    )
    got = exchange(msg, domains)
    part, node = call(
        mix_kernel,
        [
            ((variables, mesh_rows + 2 * LANES), BF, STAY),
            ((SLOTS * site_nodes.shape[1], LANES), I32, STAY),
        ],
        (feat, vmem(got), vmem(ginc), m),
        [
            wide,
            pltpu.VMEM((neighbours // 2, mesh_rows), BF),
            dma(neighbours // 2 // CHUNK),
        ],
        far=(3,),
        name="mix",
    )
    other = lax.ppermute(part, "feat", SWAP)
    (sites,) = call(
        site_kernel,
        [((mesh_rows, SLOTS * domains), BF, STAY)],
        (vmem(node),),
        scalar=False,
        name="sites",
    )
    back, own = call(
        node_kernel,
        [((rows, variables), BF, LEAVE), ((n, mesh_rows), F32, STAY)],
        (feat, vmem(part), vmem(other), vmem(ginc), m, vmem(sites), *weights),
        [
            pltpu.VMEM((inner, mesh_rows), F32),
            wide,
            pltpu.VMEM((neighbours, mesh_rows), BF),
            dma(neighbours // CHUNK),
        ],
        far=(4,),
        name="node",
    )
    got_back = exchange(back, domains)
    g, target_col = call(
        scatter_kernel,
        [
            ((mesh_rows, grid_rows), BF, COPY),
            ((site_count, 1), I32, STAY),
        ],
        (grid_t, target),
        [pltpu.VMEM((mesh_rows, grid_rows), BF), dma(8)],
        scalar=False,
        name="scatter",
    )

    def finish(*refs):
        finish_kernel(*refs, degree=degree)

    grad, site_pred = call(
        finish,
        [((n, grid_rows), F32, COPY), ((site_count, variables), BF, LEAVE)],
        (vmem(got_back), send_t, vmem(own), vmem(target_col), g),
        [
            wide,
            pltpu.VMEM((mesh_rows, 2 * HALF_DEPTH * domains), BF),
            pltpu.VMEM((mesh_rows, grid_rows), BF),
            pltpu.VMEM((n, grid_rows), F32),
            dma(8),
            dma(8),
        ],
        scalar=False,
        far=(4,),
        name="finish",
    )
    return (grad.T, site_pred)


def solution(mesh):
    return jax.shard_map(
        local,
        mesh=mesh,
        in_specs=(
            P("dom", None),
            P(),
            P(),
            P(),
            P(),
            P("dom", None),
            P("dom", None),
            P("dom", None),
            P("dom", None, None),
            P("dom", None),
            P("dom", None),
            P("dom", None),
        ),
        out_specs=(P("dom", "feat"), P("dom", None)),
        check_vma=False,
    )
```

```python
import jax
import jax.numpy as jnp
from jax import lax
from jax.experimental import pallas as pl
from jax.experimental.pallas import tpu as pltpu
from jax.sharding import PartitionSpec as P

BF = jnp.bfloat16
F32 = jnp.float32
I16 = jnp.int16
I32 = jnp.int32
LANES = 128
HALF_DEPTH = 8
SLOTS = 4
ROWS = HALF_DEPTH + SLOTS
SWAP = [(0, 1), (1, 0)]
CHUNK = 512


def dot(a, b, ca=1, cb=0):
    return lax.dot_general(a, b, (((ca,), (cb,)), ((), ())), preferred_element_type=F32)


def iota(shape, axis):
    return lax.broadcasted_iota(I32, shape, axis)


def eq_bf16(a, b):
    return jnp.where(a == b, jnp.asarray(1, BF), jnp.asarray(0, BF))


def build_counts(dst, tiles, height, lane0=0, row0=0, sub=16, unroll=4):
    cols = [[jnp.broadcast_to(r, (sub, LANES)).astype(I16) for r in rows] for rows in tiles]
    start = (iota((sub, LANES), 0) + row0).astype(I16)

    def body(i, at):
        s = pl.multiple_of(row0 + i * sub, sub)
        for t, rows in enumerate(cols):
            acc = eq_bf16(rows[0], at)
            for r in rows[1:]:
                acc = acc + eq_bf16(r, at)
            dst[pl.ds(s, sub), lane0 + t * LANES : lane0 + (t + 1) * LANES] = acc
        return at + jnp.asarray(sub, I16)

    lax.fori_loop(0, height // sub, body, start, unroll=unroll)


def build_rows(dst, index, rows, degree, block=128, unroll=2, after=None):
    start = iota((block, LANES), 1).astype(I16)
    for n, s in enumerate(range(0, rows, block)):
        cols = [
            jnp.broadcast_to(index[s : s + block, k : k + 1], (block, LANES)).astype(I16)
            for k in range(degree)
        ]

        def body(w, at, s=s, cols=cols):
            acc = eq_bf16(cols[0], at)
            for c in cols[1:]:
                acc = acc + eq_bf16(c, at)
            dst[s : s + block, pl.ds(pl.multiple_of(w * LANES, LANES), LANES)] = acc
            return at + jnp.asarray(LANES, I16)

        lax.fori_loop(0, dst.shape[1] // LANES, body, start, unroll=unroll)
        if after is not None:
            after(n)


def row_copies(src, dst, sems, starts, size, targets=None):
    targets = starts if targets is None else targets
    return [
        pltpu.make_async_copy(src.at[pl.ds(a, size), :], dst.at[pl.ds(b, size), :], sems.at[k])
        for k, (a, b) in enumerate(zip(starts, targets))
    ]


def chunks(total):
    return range(0, total, CHUNK)


def lane_tiles(rows, first=0, last=None):
    last = rows.shape[1] // LANES if last is None else last
    return [
        [rows[k : k + 1, t * LANES : (t + 1) * LANES] for k in range(rows.shape[0])]
        for t in range(first, last)
    ]


def peer_rows(k):
    return pl.ds(k, LANES, stride=ROWS)


def encode_kernel(
    inc_h, edges, send, owner, nodes, obs, msg, ginc, target, g, r, wide, inc, sem
):
    feat = lax.axis_index("feat")
    load = pltpu.make_async_copy(inc_h, inc, sem)
    load.start()
    build_counts(g, lane_tiles(edges[...]), inc.shape[0])
    picked = jnp.where(feat == 0, send[:HALF_DEPTH, :], send[HALF_DEPTH:, :])
    build_counts(r, [[picked[k : k + 1, :]] for k in range(HALF_DEPTH)], r.shape[0])
    sites = owner.shape[1]
    own = owner[...]
    member = jnp.where(iota((LANES, sites), 0) == own, 1.0, 0.0)
    member_b = member.astype(BF)
    upper = jnp.where(iota((sites, sites), 0) < iota((sites, sites), 1), 1.0, 0.0).astype(BF)
    rank = jnp.sum(dot(member_b, upper) * member, axis=0, keepdims=True)
    target[...] = rank.astype(I32) * LANES + own
    for k in range(2):
        slot = (2 * feat + k).astype(F32)
        wide[peer_rows(HALF_DEPTH + k), :] = dot(
            jnp.where(rank == slot, member, 0.0).astype(BF), obs[...]
        )
    n = nodes[...]
    high = ((n >> 5) + 1).astype(F32)
    low = (n & 31).astype(F32)
    lists = [jnp.where(rank == float(k), v, 0.0) for v in (high, low) for k in range(SLOTS)]
    lists.append(jnp.zeros((LANES - 2 * SLOTS * n.shape[0], sites), F32))
    listed = jnp.concatenate(lists, axis=0).astype(BF)
    wide[peer_rows(HALF_DEPTH + 2), :] = dot(member_b, listed, 1, 1)
    wide[peer_rows(HALF_DEPTH + 3), :] = jnp.zeros((LANES, LANES), F32)
    load.wait()
    mean = (dot(inc[...], g[...], 0, 0) * (1.0 / edges.shape[0])).astype(BF)
    ginc[...] = mean
    out = dot(mean, r[...])
    for k in range(HALF_DEPTH):
        wide[peer_rows(k), :] = out[:, k * LANES : (k + 1) * LANES].T
    msg[...] = wide[...].astype(BF)


def prepare_kernel(
    edges, mask, ginc, w_in, w_node1, w_node2, w_out, m_h, part, w_cat, w_cat_t, w_ho, w_ho_t, w_io, w_io_t, m, sems
):
    rows = edges.shape[1]
    e = edges[...]
    h = e - rows
    r = h & 15
    at = jnp.where(mask[...] > 0, jnp.where(e < rows, e, rows + r * LANES + (h >> 4)), -1)
    tiles = lane_tiles(at)
    copies = row_copies(m, m_h, sems, chunks(m.shape[0]), CHUNK)
    for row0, copy in zip(chunks(m.shape[0]), copies):
        for first in range(0, len(tiles), 4):
            build_counts(m, tiles[first : first + 4], CHUNK, first * LANES, row0)
        copy.start()
    half = rows // 2
    own = pl.ds(pl.multiple_of(lax.axis_index("feat") * half, half), half)
    part[...] = dot(ginc[:, own], m[own, :])
    width = w_in.shape[1]
    variables = w_in.shape[0]
    wi = w_in[...]
    for k in range(2):
        w1 = w_node1[k * width : (k + 1) * width, :]
        w_cat[k * variables : (k + 1) * variables, :] = dot(wi, w1).astype(BF)
        w_cat_t[:, k * variables : (k + 1) * variables] = dot(w1, wi, 0, 1).astype(BF)
    w_ho[...] = dot(w_node2[...], w_out[...]).astype(BF)
    w_ho_t[...] = dot(w_out[...], w_node2[...], 0, 1).astype(BF)
    w_io[...] = dot(wi, w_out[...]).astype(BF)
    w_io_t[...] = dot(w_out[...], wi, 0, 1).astype(BF)
    for copy in copies:
        copy.wait()


def mix_kernel(msg, own_part, m_h, part, node, wide, m, sems):
    feat = lax.axis_index("feat")
    rows = own_part.shape[1]
    count = HALF_DEPTH * LANES
    halo = rows + feat * count
    starts = [halo + k for k in chunks(count)]
    copies = row_copies(m_h, m, sems, starts, CHUNK, chunks(count))
    for copy in copies:
        copy.start()
    wide[...] = msg[...].astype(F32)
    for k in range(2):
        part[:, rows + k * LANES : rows + (k + 1) * LANES] = (
            wide[peer_rows(HALF_DEPTH + k), :].T.astype(BF)
        )
    lists = wide[peer_rows(HALF_DEPTH + 2), :].T
    n = node.shape[0]
    node[...] = ((lists[:n, :] - 1.0) * 32.0 + lists[n : 2 * n, :]).astype(I32)
    got = jnp.concatenate([wide[peer_rows(k), :].T for k in range(HALF_DEPTH)], axis=1).astype(BF)
    acc = own_part[...]
    for k, copy in zip(chunks(count), copies):
        copy.wait()
        acc = acc + dot(got[:, k : k + CHUNK], m[k : k + CHUNK, :])
    part[:, :rows] = acc.astype(BF)


def site_kernel(node, s):
    degree = node.shape[0] // SLOTS
    tiles = [[node[k * degree + j : k * degree + j + 1, :] for j in range(degree)] for k in range(SLOTS)]
    build_counts(s, tiles, s.shape[0])


def node_kernel(
    part, other, ginc, m_h, s, w_cat, w_cat_t, w_ho, w_ho_t, w_io, w_io_t, msg, own, agg_out, slope_s, wide, m, sems
):
    feat = lax.axis_index("feat")
    variables, rows = ginc.shape
    copies = row_copies(m_h, m, sems, [rows + k for k in chunks(m.shape[0])], CHUNK, chunks(m.shape[0]))
    for copy in copies:
        copy.start()
    gi = ginc[...]
    agg = (part[:, :rows].astype(F32) + other[:, :rows].astype(F32)).astype(BF)
    pre = dot(w_cat_t[...], jnp.concatenate([gi, agg], axis=0))
    sig = 1.0 / (1.0 + jnp.exp(-pre))
    hidden = (pre * sig).astype(BF)
    slope_s[...] = sig * (1.0 + pre * (1.0 - sig))
    readout = (dot(w_ho_t[...], hidden) + dot(w_io_t[...], gi)).astype(BF)
    values = dot(readout, s[...])
    mine = part[:, rows:].astype(F32)
    theirs = other[:, rows:].astype(F32)
    first = jnp.where(feat == 0, mine, theirs)
    second = jnp.where(feat == 0, theirs, mine)
    diff = (values - jnp.concatenate([first, second], axis=1)).astype(BF)
    d = dot(diff, s[...], 1, 1).astype(BF)
    inner = (dot(w_ho[...], d) * slope_s[...]).astype(BF)
    n = variables // 2
    cols = pl.ds(pl.multiple_of(feat * n, n), n)
    agg_cols = pl.ds(pl.multiple_of(variables + feat * n, n), n)
    both = dot(jnp.concatenate([w_cat[cols, :], w_cat[agg_cols, :]], axis=0), inner)
    agg_grad = both[n:, :].T.astype(BF)
    agg_out[...] = agg_grad
    own[...] = dot(w_io[cols, :], d) + both[:n, :]
    site_rows = values.T
    for k in range(SLOTS):
        wide[peer_rows(HALF_DEPTH + k), :] = site_rows[k * LANES : (k + 1) * LANES, :]
    for copy in copies:
        copy.wait()
    count = HALF_DEPTH * LANES
    low = dot(m[:count, :], agg_grad)
    high = dot(m[count:, :], agg_grad)
    halo = jnp.concatenate([low, high], axis=1)
    for k in range(HALF_DEPTH):
        wide[peer_rows(k), :] = halo[k * LANES : (k + 1) * LANES, :]
    msg[...] = wide[...].astype(BF)


def scatter_kernel(
    edges, target, send, own_in, agg_grad, m_h, g_h, near, target_col, send_out, own, g, m, sems, m_sem
):
    load = pltpu.make_async_copy(m_h.at[pl.ds(0, m.shape[0]), :], m, m_sem)
    load.start()
    send_out[...] = send[...]
    target_col[...] = jnp.broadcast_to(target[...], (8, target.shape[1])).T[:, :1]
    e = edges[...]
    columns = jnp.concatenate([e, e], axis=0).T
    block = g.shape[0] // sems.shape[0]
    copies = row_copies(g, g_h, sems, range(0, g.shape[0], block), block)
    build_rows(g, columns, g.shape[0], e.shape[0], block, after=lambda n: copies[n].start())
    build_rows(near, columns - g.shape[1], near.shape[0], e.shape[0], block)
    load.wait()
    own[...] = own_in[...] + dot(m[...], agg_grad[...]).T
    for copy in copies:
        copy.wait()


def finish_kernel(
    msg, send, own, target, near, g_h, out_h, pred, wide, r, g, out, in_sems, out_sems, *, degree
):
    far = g.shape[1]
    spans = [pl.ds(k, CHUNK) for k in chunks(far + near.shape[1])]
    loads = [
        pltpu.make_async_copy(g_h.at[:, at], g.at[:, at], in_sems.at[k])
        for k, at in enumerate(spans[: far // CHUNK])
    ]
    stores = [
        pltpu.make_async_copy(out.at[:, at], out_h.at[:, at], out_sems.at[k])
        for k, at in enumerate(spans)
    ]
    for load in loads:
        load.start()
    depth = send.shape[0]
    build_counts(r, [[send[k : k + 1, :]] for k in range(depth)], r.shape[0], unroll=2)
    wide[...] = msg[...].astype(F32)
    back = jnp.concatenate([wide[peer_rows(k), :] for k in range(HALF_DEPTH)], axis=0).astype(BF)
    count = back.shape[0]
    n = own.shape[0]
    low = dot(r[:, :count], back).T
    high = dot(r[:, count:], back).T
    grad = ((own[...] + low[:n, :] + high[n:, :]) * (1.0 / degree)).astype(BF)
    slots = [wide[peer_rows(HALF_DEPTH + k), :] for k in range(SLOTS)]
    pick = jnp.where(target[...] == iota((target.shape[0], SLOTS * LANES), 1), 1.0, 0.0).astype(BF)
    pred[...] = dot(pick, jnp.concatenate(slots, axis=0).astype(BF)).astype(BF)
    out[:, far:] = dot(grad, near[...])
    stores[-1].start()
    for at, load, store in zip(spans, loads, stores):
        load.wait()
        out[:, at] = dot(grad, g[:, at])
        store.start()
    for store in stores:
        store.wait()


FULL = pl.BlockSpec(memory_space=pltpu.VMEM)
HBM = pl.BlockSpec(memory_space=pl.ANY)
STAY, LEAVE, COPY = "stay", "leave", "copy"


def vmem(x):
    return pltpu.with_memory_space_constraint(x, pltpu.VMEM)


def dma(n):
    return pltpu.SemaphoreType.DMA((n,))


def call(kernel, outs, args, scratch=(), far=(), name=None):
    return pl.pallas_call(
        kernel,
        out_shape=[
            pltpu.VMEM(s, t) if where == STAY else jax.ShapeDtypeStruct(s, t) for s, t, where in outs
        ],
        in_specs=[HBM if k in far else FULL for k in range(len(args))],
        out_specs=[HBM if where == COPY else FULL for _, _, where in outs],
        scratch_shapes=list(scratch),
        name=name,
    )(*args)


def exchange(msg, domains):
    x = msg.reshape(domains, ROWS // 4, 4, msg.shape[1])
    x = lax.all_to_all(x, "dom", split_axis=0, concat_axis=0, tiled=True)
    return x.reshape(msg.shape)


def local(
    increments,
    w_in,
    w_node1,
    w_node2,
    w_out,
    grid_edges,
    mesh_edges,
    mesh_mask,
    send_rows,
    site_owner,
    site_nodes,
    site_obs,
):
    domains = lax.axis_size("dom")
    grid_rows, variables = increments.shape
    mesh_rows = mesh_edges.shape[0]
    inner = w_node2.shape[0]
    site_count = site_obs.shape[0]
    rows = domains * ROWS
    degree = grid_edges.shape[1]
    n = variables // 2
    neighbours = mesh_rows + 2 * HALF_DEPTH * domains
    wide = pltpu.VMEM((rows, variables), F32)
    grid_t = grid_edges.T
    send_t = send_rows[0].T
    msg, ginc, target = call(
        encode_kernel,
        [
            ((rows, variables), BF, LEAVE),
            ((variables, mesh_rows), BF, STAY),
            ((1, site_count), I32, LEAVE),
        ],
        (increments, grid_t, send_t, site_owner.T, site_nodes.T, site_obs),
        [
            pltpu.VMEM((grid_rows, mesh_rows), BF),
            pltpu.VMEM((mesh_rows, HALF_DEPTH * domains), BF),
            wide,
            pltpu.VMEM((grid_rows, variables), BF),
            pltpu.SemaphoreType.DMA,
        ],
        far=(0,),
        name="encode",
    )
    m, own_part, *weights = call(
        prepare_kernel,
        [
            ((neighbours, mesh_rows), BF, COPY),
            ((variables, mesh_rows), F32, STAY),
            ((2 * variables, inner), BF, LEAVE),
            ((inner, 2 * variables), BF, LEAVE),
            ((inner, variables), BF, LEAVE),
            ((variables, inner), BF, LEAVE),
            ((variables, variables), BF, LEAVE),
            ((variables, variables), BF, LEAVE),
        ],
        (mesh_edges.T, mesh_mask.T, vmem(ginc), w_in, w_node1, w_node2, w_out),
        [pltpu.VMEM((neighbours, mesh_rows), BF), dma(neighbours // CHUNK)],
        name="prepare",
    )
    got = exchange(msg, domains)
    part, node = call(
        mix_kernel,
        [
            ((variables, mesh_rows + 2 * LANES), BF, STAY),
            ((SLOTS * site_nodes.shape[1], LANES), I32, STAY),
        ],
        (vmem(got), vmem(own_part), m),
        [
            wide,
            pltpu.VMEM((HALF_DEPTH * domains, mesh_rows), BF),
            dma(HALF_DEPTH * domains // CHUNK),
        ],
        far=(2,),
        name="mix",
    )
    other = lax.ppermute(part, "feat", SWAP)
    (sites,) = call(
        site_kernel,
        [((mesh_rows, SLOTS * domains), BF, STAY)],
        (vmem(node),),
        name="sites",
    )
    back, own, agg_grad = call(
        node_kernel,
        [
            ((rows, variables), BF, LEAVE),
            ((n, mesh_rows), F32, LEAVE),
            ((mesh_rows, n), BF, LEAVE),
        ],
        (vmem(part), vmem(other), vmem(ginc), m, vmem(sites), *weights),
        [
            pltpu.VMEM((inner, mesh_rows), F32),
            wide,
            pltpu.VMEM((neighbours - mesh_rows, mesh_rows), BF),
            dma((neighbours - mesh_rows) // CHUNK),
        ],
        far=(3,),
        name="node",
    )
    got_back = exchange(back, domains)
    far = grid_rows - CHUNK
    g, near, target_col, send_near, own = call(
        scatter_kernel,
        [
            ((mesh_rows, far), BF, COPY),
            ((mesh_rows, CHUNK), BF, STAY),
            ((site_count, 1), I32, STAY),
            (send_t.shape, I32, STAY),
            ((n, mesh_rows), F32, STAY),
        ],
        (grid_t, target, send_t, own, agg_grad, m),
        [
            pltpu.VMEM((mesh_rows, far), BF),
            pltpu.VMEM((mesh_rows, mesh_rows), BF),
            dma(8),
            pltpu.SemaphoreType.DMA,
        ],
        far=(5,),
        name="scatter",
    )

    def finish(*refs):
        finish_kernel(*refs, degree=degree)

    grad, site_pred = call(
        finish,
        [((n, grid_rows), F32, COPY), ((site_count, variables), BF, LEAVE)],
        (vmem(got_back), vmem(send_near), vmem(own), vmem(target_col), vmem(near), g),
        [
            wide,
            pltpu.VMEM((mesh_rows, 2 * HALF_DEPTH * domains), BF),
            pltpu.VMEM((mesh_rows, far), BF),
            pltpu.VMEM((n, grid_rows), F32),
            dma(far // CHUNK),
            dma(grid_rows // CHUNK),
        ],
        far=(5,),
        name="finish",
    )
    return (grad.T, site_pred)


def solution(mesh):
    return jax.shard_map(
        local,
        mesh=mesh,
        in_specs=(
            P("dom", None),
            P(),
            P(),
            P(),
            P(),
            P("dom", None),
            P("dom", None),
            P("dom", None),
            P("dom", None, None),
            P("dom", None),
            P("dom", None),
            P("dom", None),
        ),
        out_specs=(P("dom", "feat"), P("dom", None)),
        check_vma=False,
    )
```

```python
import jax
import jax.numpy as jnp
from jax import lax
from jax.experimental import pallas as pl
from jax.experimental.pallas import tpu as pltpu
from jax.sharding import PartitionSpec as P

BF = jnp.bfloat16
F32 = jnp.float32
I16 = jnp.int16
I32 = jnp.int32
LANES = 128
HALF_DEPTH = 8
SLOTS = 4
ROWS = HALF_DEPTH + SLOTS
SWAP = [(0, 1), (1, 0)]
PIECES = 2
CHUNK = 512


def dot(a, b, ca=1, cb=0):
    return lax.dot_general(a, b, (((ca,), (cb,)), ((), ())), preferred_element_type=F32)


def iota(shape, axis):
    return lax.broadcasted_iota(I32, shape, axis)


def eq_bf16(a, b):
    return jnp.where(a == b, jnp.asarray(1, BF), jnp.asarray(0, BF))


def build_counts(dst, tiles, height, lane0=0, row0=0, sub=16, unroll=4):
    cols = [[jnp.broadcast_to(r, (sub, LANES)).astype(I16) for r in rows] for rows in tiles]
    start = (iota((sub, LANES), 0) + row0).astype(I16)

    def body(i, at):
        s = pl.multiple_of(row0 + i * sub, sub)
        for t, rows in enumerate(cols):
            acc = eq_bf16(rows[0], at)
            for r in rows[1:]:
                acc = acc + eq_bf16(r, at)
            dst[pl.ds(s, sub), lane0 + t * LANES : lane0 + (t + 1) * LANES] = acc
        return at + jnp.asarray(sub, I16)

    lax.fori_loop(0, height // sub, body, start, unroll=unroll)


def build_rows(dst, index, rows, degree, block=128, unroll=2, after=None):
    start = iota((block, LANES), 1).astype(I16)
    for n, s in enumerate(range(0, rows, block)):
        cols = [
            jnp.broadcast_to(index[s : s + block, k : k + 1], (block, LANES)).astype(I16)
            for k in range(degree)
        ]

        def body(w, at, s=s, cols=cols):
            acc = eq_bf16(cols[0], at)
            for c in cols[1:]:
                acc = acc + eq_bf16(c, at)
            dst[s : s + block, pl.ds(pl.multiple_of(w * LANES, LANES), LANES)] = acc
            return at + jnp.asarray(LANES, I16)

        lax.fori_loop(0, dst.shape[1] // LANES, body, start, unroll=unroll)
        if after is not None:
            after(n)


def row_copies(src, dst, sems, starts, size, targets=None):
    targets = starts if targets is None else targets
    return [
        pltpu.make_async_copy(src.at[pl.ds(a, size), :], dst.at[pl.ds(b, size), :], sems.at[k])
        for k, (a, b) in enumerate(zip(starts, targets))
    ]


def chunks(total):
    return range(0, total, CHUNK)


def lane_tiles(rows, first=0, last=None):
    last = rows.shape[1] // LANES if last is None else last
    return [
        [rows[k : k + 1, t * LANES : (t + 1) * LANES] for k in range(rows.shape[0])]
        for t in range(first, last)
    ]


def peer_rows(k):
    return pl.ds(k, LANES, stride=ROWS)


def encode_kernel(
    inc_h, edges, send, owner, nodes, obs, msg, ginc, target, g, r, wide, inc, sem
):
    feat = lax.axis_index("feat")
    load = pltpu.make_async_copy(inc_h, inc, sem)
    load.start()
    build_counts(g, lane_tiles(edges[...]), inc.shape[0])
    picked = jnp.where(feat == 0, send[:HALF_DEPTH, :], send[HALF_DEPTH:, :])
    build_counts(r, [[picked[k : k + 1, :]] for k in range(HALF_DEPTH)], r.shape[0])
    sites = owner.shape[1]
    own = owner[...]
    member = jnp.where(iota((LANES, sites), 0) == own, 1.0, 0.0)
    member_b = member.astype(BF)
    upper = jnp.where(iota((sites, sites), 0) < iota((sites, sites), 1), 1.0, 0.0).astype(BF)
    rank = jnp.sum(dot(member_b, upper) * member, axis=0, keepdims=True)
    target[...] = rank.astype(I32) * LANES + own
    for k in range(2):
        slot = (2 * feat + k).astype(F32)
        wide[peer_rows(HALF_DEPTH + k), :] = dot(
            jnp.where(rank == slot, member, 0.0).astype(BF), obs[...]
        )
    n = nodes[...]
    high = ((n >> 5) + 1).astype(F32)
    low = (n & 31).astype(F32)
    lists = [jnp.where(rank == float(k), v, 0.0) for v in (high, low) for k in range(SLOTS)]
    lists.append(jnp.zeros((LANES - 2 * SLOTS * n.shape[0], sites), F32))
    listed = jnp.concatenate(lists, axis=0).astype(BF)
    wide[peer_rows(HALF_DEPTH + 2), :] = dot(member_b, listed, 1, 1)
    wide[peer_rows(HALF_DEPTH + 3), :] = jnp.zeros((LANES, LANES), F32)
    load.wait()
    mean = (dot(inc[...], g[...], 0, 0) * (1.0 / edges.shape[0])).astype(BF)
    ginc[...] = mean
    out = dot(mean, r[...])
    for k in range(HALF_DEPTH):
        wide[peer_rows(k), :] = out[:, k * LANES : (k + 1) * LANES].T
    msg[...] = wide[...].astype(BF)


def prepare_kernel(
    edges, mask, ginc, w_in, w_node1, w_node2, w_out, m_h, part, w_cat, w_cat_t, w_ho, w_ho_t, w_io, w_io_t, m, sems
):
    rows = edges.shape[1]
    e = edges[...]
    h = e - rows
    r = h & 15
    at = jnp.where(mask[...] > 0, jnp.where(e < rows, e, rows + r * LANES + (h >> 4)), -1)
    tiles = lane_tiles(at)
    copies = row_copies(m, m_h, sems, chunks(m.shape[0]), CHUNK)
    for row0, copy in zip(chunks(m.shape[0]), copies):
        for first in range(0, len(tiles), 4):
            build_counts(m, tiles[first : first + 4], CHUNK, first * LANES, row0)
        copy.start()
    half = rows // 2
    own = pl.ds(pl.multiple_of(lax.axis_index("feat") * half, half), half)
    part[...] = dot(ginc[:, own], m[own, :])
    width = w_in.shape[1]
    variables = w_in.shape[0]
    wi = w_in[...]
    for k in range(2):
        w1 = w_node1[k * width : (k + 1) * width, :]
        w_cat[k * variables : (k + 1) * variables, :] = dot(wi, w1).astype(BF)
        w_cat_t[:, k * variables : (k + 1) * variables] = dot(w1, wi, 0, 1).astype(BF)
    w_ho[...] = dot(w_node2[...], w_out[...]).astype(BF)
    w_ho_t[...] = dot(w_out[...], w_node2[...], 0, 1).astype(BF)
    w_io[...] = dot(wi, w_out[...]).astype(BF)
    w_io_t[...] = dot(w_out[...], wi, 0, 1).astype(BF)
    for copy in copies:
        copy.wait()


def mix_kernel(msg, own_part, m_h, part, node, wide, m, sems):
    feat = lax.axis_index("feat")
    rows = own_part.shape[1]
    count = HALF_DEPTH * LANES
    halo = rows + feat * count
    starts = [halo + k for k in chunks(count)]
    copies = row_copies(m_h, m, sems, starts, CHUNK, chunks(count))
    for copy in copies:
        copy.start()
    wide[...] = msg[...].astype(F32)
    for k in range(2):
        part[:, rows + k * LANES : rows + (k + 1) * LANES] = (
            wide[peer_rows(HALF_DEPTH + k), :].T.astype(BF)
        )
    lists = wide[peer_rows(HALF_DEPTH + 2), :].T
    n = node.shape[0]
    node[...] = ((lists[:n, :] - 1.0) * 32.0 + lists[n : 2 * n, :]).astype(I32)
    got = jnp.concatenate([wide[peer_rows(k), :].T for k in range(HALF_DEPTH)], axis=1).astype(BF)
    acc = own_part[...]
    for k, copy in zip(chunks(count), copies):
        copy.wait()
        acc = acc + dot(got[:, k : k + CHUNK], m[k : k + CHUNK, :])
    part[:, :rows] = acc.astype(BF)


def site_kernel(node, s):
    degree = node.shape[0] // SLOTS
    tiles = [[node[k * degree + j : k * degree + j + 1, :] for j in range(degree)] for k in range(SLOTS)]
    build_counts(s, tiles, s.shape[0])


def node_kernel(
    part,
    other,
    ginc,
    m_h,
    s,
    w_cat_h,
    w_cat_t,
    w_ho_h,
    w_ho_t,
    w_io_h,
    w_io_t,
    msg,
    own,
    agg_out,
    slope_s,
    wide,
    m,
    sems,
    w_cat,
    w_ho,
    w_io,
    w_sems,
):
    feat = lax.axis_index("feat")
    variables, rows = ginc.shape
    late = [
        pltpu.make_async_copy(a, b, w_sems.at[k])
        for k, (a, b) in enumerate(((w_ho_h, w_ho), (w_cat_h, w_cat), (w_io_h, w_io)))
    ]
    for copy in late:
        copy.start()
    copies = row_copies(m_h, m, sems, [rows + k for k in chunks(m.shape[0])], CHUNK, chunks(m.shape[0]))
    for copy in copies:
        copy.start()
    gi = ginc[...]
    agg = (part[:, :rows].astype(F32) + other[:, :rows].astype(F32)).astype(BF)
    pre = dot(w_cat_t[...], jnp.concatenate([gi, agg], axis=0))
    sig = 1.0 / (1.0 + jnp.exp(-pre))
    hidden = (pre * sig).astype(BF)
    slope_s[...] = sig * (1.0 + pre * (1.0 - sig))
    readout = (dot(w_ho_t[...], hidden) + dot(w_io_t[...], gi)).astype(BF)
    values = dot(readout, s[...])
    mine = part[:, rows:].astype(F32)
    theirs = other[:, rows:].astype(F32)
    first = jnp.where(feat == 0, mine, theirs)
    second = jnp.where(feat == 0, theirs, mine)
    diff = (values - jnp.concatenate([first, second], axis=1)).astype(BF)
    d = dot(diff, s[...], 1, 1).astype(BF)
    for copy in late:
        copy.wait()
    inner = (dot(w_ho[...], d) * slope_s[...]).astype(BF)
    n = variables // 2
    cols = pl.ds(pl.multiple_of(feat * n, n), n)
    agg_cols = pl.ds(pl.multiple_of(variables + feat * n, n), n)
    both = dot(jnp.concatenate([w_cat[cols, :], w_cat[agg_cols, :]], axis=0), inner)
    agg_grad = both[n:, :].T.astype(BF)
    agg_out[...] = agg_grad
    own[...] = dot(w_io[cols, :], d) + both[:n, :]
    site_rows = values.T
    for k in range(SLOTS):
        wide[peer_rows(HALF_DEPTH + k), :] = site_rows[k * LANES : (k + 1) * LANES, :]
    for copy in copies:
        copy.wait()
    count = HALF_DEPTH * LANES
    low = dot(m[:count, :], agg_grad)
    high = dot(m[count:, :], agg_grad)
    halo = jnp.concatenate([low, high], axis=1)
    for k in range(HALF_DEPTH):
        wide[peer_rows(k), :] = halo[k * LANES : (k + 1) * LANES, :]
    msg[...] = wide[...].astype(BF)


def scatter_kernel(
    edges, target, send, own_in, agg_grad, m_h, g_h, near, target_col, send_out, own, g, m, sems, m_sem
):
    load = pltpu.make_async_copy(m_h.at[pl.ds(0, m.shape[0]), :], m, m_sem)
    load.start()
    send_out[...] = send[...]
    target_col[...] = jnp.broadcast_to(target[...], (8, target.shape[1])).T[:, :1]
    e = edges[...]
    columns = jnp.concatenate([e, e], axis=0).T
    block = g.shape[0] // sems.shape[0]
    copies = row_copies(g, g_h, sems, range(0, g.shape[0], block), block)
    build_rows(g, columns, g.shape[0], e.shape[0], block, after=lambda n: copies[n].start())
    build_rows(near, columns - g.shape[1], near.shape[0], e.shape[0], block)
    load.wait()
    own[...] = own_in[...] + dot(m[...], agg_grad[...]).T
    for copy in copies:
        copy.wait()


def finish_kernel(
    msg, send, own, target, near, g_h, out_h, pred, wide, r, g, out, in_sems, out_sems, *, degree
):
    far = g.shape[1]
    piece = far // PIECES
    spans = [(k, piece) for k in range(0, far, piece)] + [(far, near.shape[1])]
    spans = [pl.ds(*span) for span in spans]
    loads = [
        pltpu.make_async_copy(g_h.at[:, at], g.at[:, at], in_sems.at[k])
        for k, at in enumerate(spans[:-1])
    ]
    stores = [
        pltpu.make_async_copy(out.at[:, at], out_h.at[:, at], out_sems.at[k])
        for k, at in enumerate(spans)
    ]
    for load in loads:
        load.start()
    depth = send.shape[0]
    build_counts(r, [[send[k : k + 1, :]] for k in range(depth)], r.shape[0], unroll=2)
    wide[...] = msg[...].astype(F32)
    back = jnp.concatenate([wide[peer_rows(k), :] for k in range(HALF_DEPTH)], axis=0).astype(BF)
    count = back.shape[0]
    n = own.shape[0]
    low = dot(r[:, :count], back).T
    high = dot(r[:, count:], back).T
    grad = ((own[...] + low[:n, :] + high[n:, :]) * (1.0 / degree)).astype(BF)
    slots = [wide[peer_rows(HALF_DEPTH + k), :] for k in range(SLOTS)]
    pick = jnp.where(target[...] == iota((target.shape[0], SLOTS * LANES), 1), 1.0, 0.0).astype(BF)
    pred[...] = dot(pick, jnp.concatenate(slots, axis=0).astype(BF)).astype(BF)
    out[:, far:] = dot(grad, near[...])
    stores[-1].start()
    for at, load, store in zip(spans, loads, stores):
        load.wait()
        out[:, at] = dot(grad, g[:, at])
        store.start()
    for store in stores:
        store.wait()


FULL = pl.BlockSpec(memory_space=pltpu.VMEM)
HBM = pl.BlockSpec(memory_space=pl.ANY)
STAY, LEAVE, COPY = "stay", "leave", "copy"


def vmem(x):
    return pltpu.with_memory_space_constraint(x, pltpu.VMEM)


def dma(n):
    return pltpu.SemaphoreType.DMA((n,))


def call(kernel, outs, args, scratch=(), far=(), name=None):
    return pl.pallas_call(
        kernel,
        out_shape=[
            pltpu.VMEM(s, t) if where == STAY else jax.ShapeDtypeStruct(s, t) for s, t, where in outs
        ],
        in_specs=[HBM if k in far else FULL for k in range(len(args))],
        out_specs=[HBM if where == COPY else FULL for _, _, where in outs],
        scratch_shapes=list(scratch),
        name=name,
    )(*args)


def exchange(msg, domains):
    x = msg.reshape(domains, ROWS // 4, 4, msg.shape[1])
    x = lax.all_to_all(x, "dom", split_axis=0, concat_axis=0, tiled=True)
    return x.reshape(msg.shape)


def local(
    increments,
    w_in,
    w_node1,
    w_node2,
    w_out,
    grid_edges,
    mesh_edges,
    mesh_mask,
    send_rows,
    site_owner,
    site_nodes,
    site_obs,
):
    domains = lax.axis_size("dom")
    grid_rows, variables = increments.shape
    mesh_rows = mesh_edges.shape[0]
    inner = w_node2.shape[0]
    site_count = site_obs.shape[0]
    rows = domains * ROWS
    degree = grid_edges.shape[1]
    n = variables // 2
    neighbours = mesh_rows + 2 * HALF_DEPTH * domains
    wide = pltpu.VMEM((rows, variables), F32)
    grid_t = grid_edges.T
    send_t = send_rows[0].T
    msg, ginc, target = call(
        encode_kernel,
        [
            ((rows, variables), BF, LEAVE),
            ((variables, mesh_rows), BF, STAY),
            ((1, site_count), I32, LEAVE),
        ],
        (increments, grid_t, send_t, site_owner.T, site_nodes.T, site_obs),
        [
            pltpu.VMEM((grid_rows, mesh_rows), BF),
            pltpu.VMEM((mesh_rows, HALF_DEPTH * domains), BF),
            wide,
            pltpu.VMEM((grid_rows, variables), BF),
            pltpu.SemaphoreType.DMA,
        ],
        far=(0,),
        name="encode",
    )
    m, own_part, *weights = call(
        prepare_kernel,
        [
            ((neighbours, mesh_rows), BF, COPY),
            ((variables, mesh_rows), F32, STAY),
            ((2 * variables, inner), BF, LEAVE),
            ((inner, 2 * variables), BF, STAY),
            ((inner, variables), BF, LEAVE),
            ((variables, inner), BF, STAY),
            ((variables, variables), BF, LEAVE),
            ((variables, variables), BF, STAY),
        ],
        (mesh_edges.T, mesh_mask.T, vmem(ginc), w_in, w_node1, w_node2, w_out),
        [pltpu.VMEM((neighbours, mesh_rows), BF), dma(neighbours // CHUNK)],
        name="prepare",
    )
    got = exchange(msg, domains)
    part, node = call(
        mix_kernel,
        [
            ((variables, mesh_rows + 2 * LANES), BF, STAY),
            ((SLOTS * site_nodes.shape[1], LANES), I32, STAY),
        ],
        (vmem(got), vmem(own_part), m),
        [
            wide,
            pltpu.VMEM((HALF_DEPTH * domains, mesh_rows), BF),
            dma(HALF_DEPTH * domains // CHUNK),
        ],
        far=(2,),
        name="mix",
    )
    other = lax.ppermute(part, "feat", SWAP)
    (sites,) = call(
        site_kernel,
        [((mesh_rows, SLOTS * domains), BF, STAY)],
        (vmem(node),),
        name="sites",
    )
    back, own, agg_grad = call(
        node_kernel,
        [
            ((rows, variables), BF, LEAVE),
            ((n, mesh_rows), F32, LEAVE),
            ((mesh_rows, n), BF, LEAVE),
        ],
        (
            vmem(part),
            vmem(other),
            vmem(ginc),
            m,
            vmem(sites),
            *[vmem(w) if k % 2 else w for k, w in enumerate(weights)],
        ),
        [
            pltpu.VMEM((inner, mesh_rows), F32),
            wide,
            pltpu.VMEM((neighbours - mesh_rows, mesh_rows), BF),
            dma((neighbours - mesh_rows) // CHUNK),
            *[pltpu.VMEM(w.shape, BF) for w in (weights[0], weights[2], weights[4])],
            dma(3),
        ],
        far=(3, 5, 7, 9),
        name="node",
    )
    got_back = exchange(back, domains)
    near_cells = 3 * CHUNK // 2
    far = grid_rows - near_cells
    g, near, target_col, send_near, own = call(
        scatter_kernel,
        [
            ((mesh_rows, far), BF, COPY),
            ((mesh_rows, near_cells), BF, STAY),
            ((site_count, 1), I32, STAY),
            (send_t.shape, I32, STAY),
            ((n, mesh_rows), F32, STAY),
        ],
        (grid_t, target, send_t, own, agg_grad, m),
        [
            pltpu.VMEM((mesh_rows, far), BF),
            pltpu.VMEM((mesh_rows, mesh_rows), BF),
            dma(8),
            pltpu.SemaphoreType.DMA,
        ],
        far=(5,),
        name="scatter",
    )

    def finish(*refs):
        finish_kernel(*refs, degree=degree)

    grad, site_pred = call(
        finish,
        [((n, grid_rows), F32, COPY), ((site_count, variables), BF, LEAVE)],
        (vmem(got_back), vmem(send_near), vmem(own), vmem(target_col), vmem(near), g),
        [
            wide,
            pltpu.VMEM((mesh_rows, 2 * HALF_DEPTH * domains), BF),
            pltpu.VMEM((mesh_rows, far), BF),
            pltpu.VMEM((n, grid_rows), F32),
            dma(PIECES),
            dma(PIECES + 1),
        ],
        far=(5,),
        name="finish",
    )
    return (grad.T, site_pred)


def solution(mesh):
    return jax.shard_map(
        local,
        mesh=mesh,
        in_specs=(
            P("dom", None),
            P(),
            P(),
            P(),
            P(),
            P("dom", None),
            P("dom", None),
            P("dom", None),
            P("dom", None, None),
            P("dom", None),
            P("dom", None),
            P("dom", None),
        ),
        out_specs=(P("dom", "feat"), P("dom", None)),
        check_vma=False,
    )
```

```python
import jax
import jax.numpy as jnp
from jax import lax
from jax.experimental import pallas as pl
from jax.experimental.pallas import tpu as pltpu
from jax.sharding import PartitionSpec as P

BF = jnp.bfloat16
F32 = jnp.float32
I16 = jnp.int16
I32 = jnp.int32
LANES = 128
HALF_DEPTH = 8
SLOTS = 4
ROWS = HALF_DEPTH + SLOTS
SWAP = [(0, 1), (1, 0)]
PIECES = 2
CHUNK = 512


def dot(a, b, ca=1, cb=0):
    return lax.dot_general(a, b, (((ca,), (cb,)), ((), ())), preferred_element_type=F32)


def iota(shape, axis):
    return lax.broadcasted_iota(I32, shape, axis)


def eq_bf16(a, b):
    return jnp.where(a == b, jnp.asarray(1, BF), jnp.asarray(0, BF))


def build_counts(dst, tiles, height, lane0=0, row0=0, sub=16, unroll=4):
    cols = [[jnp.broadcast_to(r, (sub, LANES)).astype(I16) for r in rows] for rows in tiles]
    start = (iota((sub, LANES), 0) + row0).astype(I16)

    def body(i, at):
        s = pl.multiple_of(row0 + i * sub, sub)
        for t, rows in enumerate(cols):
            acc = eq_bf16(rows[0], at)
            for r in rows[1:]:
                acc = acc + eq_bf16(r, at)
            dst[pl.ds(s, sub), lane0 + t * LANES : lane0 + (t + 1) * LANES] = acc
        return at + jnp.asarray(sub, I16)

    lax.fori_loop(0, height // sub, body, start, unroll=unroll)


def build_rows(dst, index, rows, degree, block=128, unroll=2, after=None):
    start = iota((block, LANES), 1).astype(I16)
    for n, s in enumerate(range(0, rows, block)):
        cols = [
            jnp.broadcast_to(index[s : s + block, k : k + 1], (block, LANES)).astype(I16)
            for k in range(degree)
        ]

        def body(w, at, s=s, cols=cols):
            acc = eq_bf16(cols[0], at)
            for c in cols[1:]:
                acc = acc + eq_bf16(c, at)
            dst[s : s + block, pl.ds(pl.multiple_of(w * LANES, LANES), LANES)] = acc
            return at + jnp.asarray(LANES, I16)

        lax.fori_loop(0, dst.shape[1] // LANES, body, start, unroll=unroll)
        if after is not None:
            after(n)


def row_copies(src, dst, sems, starts, size, targets=None):
    targets = starts if targets is None else targets
    return [
        pltpu.make_async_copy(src.at[pl.ds(a, size), :], dst.at[pl.ds(b, size), :], sems.at[k])
        for k, (a, b) in enumerate(zip(starts, targets))
    ]


def chunks(total):
    return range(0, total, CHUNK)


def lane_tiles(rows, first=0, last=None):
    last = rows.shape[1] // LANES if last is None else last
    return [
        [rows[k : k + 1, t * LANES : (t + 1) * LANES] for k in range(rows.shape[0])]
        for t in range(first, last)
    ]


def peer_rows(k):
    return pl.ds(k, LANES, stride=ROWS)


def encode_kernel(
    inc_h, edges, *refs
):
    small_h, (msg, ginc, target, g, r, wide, inc, sem), (*small, sems) = refs[:4], refs[4:12], refs[12:]
    send, owner, nodes, obs = small
    feat = lax.axis_index("feat")
    load = pltpu.make_async_copy(inc_h, inc, sem)
    late = [pltpu.make_async_copy(a, b, sems.at[k]) for k, (a, b) in enumerate(zip(small_h, small))]
    for copy in late:
        copy.start()
    load.start()
    build_counts(g, lane_tiles(edges[...]), inc.shape[0], unroll=8)
    for copy in late:
        copy.wait()
    picked = jnp.where(feat == 0, send[:HALF_DEPTH, :], send[HALF_DEPTH:, :])
    build_counts(r, [[picked[k : k + 1, :]] for k in range(HALF_DEPTH)], r.shape[0])
    sites = owner.shape[1]
    own = owner[...]
    member = jnp.where(iota((LANES, sites), 0) == own, 1.0, 0.0)
    member_b = member.astype(BF)
    upper = jnp.where(iota((sites, sites), 0) < iota((sites, sites), 1), 1.0, 0.0).astype(BF)
    rank = jnp.sum(dot(member_b, upper) * member, axis=0, keepdims=True)
    target[...] = rank.astype(I32) * LANES + own
    for k in range(2):
        slot = (2 * feat + k).astype(F32)
        wide[peer_rows(HALF_DEPTH + k), :] = dot(
            jnp.where(rank == slot, member, 0.0).astype(BF), obs[...]
        )
    n = nodes[...]
    high = ((n >> 5) + 1).astype(F32)
    low = (n & 31).astype(F32)
    lists = [jnp.where(rank == float(k), v, 0.0) for v in (high, low) for k in range(SLOTS)]
    lists.append(jnp.zeros((LANES - 2 * SLOTS * n.shape[0], sites), F32))
    listed = jnp.concatenate(lists, axis=0).astype(BF)
    wide[peer_rows(HALF_DEPTH + 2), :] = dot(member_b, listed, 1, 1)
    wide[peer_rows(HALF_DEPTH + 3), :] = jnp.zeros((LANES, LANES), F32)
    load.wait()
    mean = (dot(inc[...], g[...], 0, 0) * (1.0 / edges.shape[0])).astype(BF)
    ginc[...] = mean
    out = dot(mean, r[...])
    for k in range(HALF_DEPTH):
        wide[peer_rows(k), :] = out[:, k * LANES : (k + 1) * LANES].T
    msg[...] = wide[...].astype(BF)


def prepare_kernel(
    edges, mask, ginc, w_in, w_node1, w_node2, w_out, m_h, part, w_cat, w_cat_t, w_ho, w_ho_t, w_io, w_io_t, m, sems
):
    rows = edges.shape[1]
    e = edges[...]
    h = e - rows
    r = h & 15
    at = jnp.where(mask[...] > 0, jnp.where(e < rows, e, rows + r * LANES + (h >> 4)), -1)
    tiles = lane_tiles(at)
    copies = row_copies(m, m_h, sems, chunks(m.shape[0]), CHUNK)
    for row0, copy in zip(chunks(m.shape[0]), copies):
        for first in range(0, len(tiles), 4):
            build_counts(m, tiles[first : first + 4], CHUNK, first * LANES, row0)
        copy.start()
    half = rows // 2
    own = pl.ds(pl.multiple_of(lax.axis_index("feat") * half, half), half)
    part[...] = dot(ginc[:, own], m[own, :])
    width = w_in.shape[1]
    variables = w_in.shape[0]
    wi = w_in[...]
    for k in range(2):
        w1 = w_node1[k * width : (k + 1) * width, :]
        w_cat[k * variables : (k + 1) * variables, :] = dot(wi, w1).astype(BF)
        w_cat_t[:, k * variables : (k + 1) * variables] = dot(w1, wi, 0, 1).astype(BF)
    w_ho[...] = dot(w_node2[...], w_out[...]).astype(BF)
    w_ho_t[...] = dot(w_out[...], w_node2[...], 0, 1).astype(BF)
    w_io[...] = dot(wi, w_out[...]).astype(BF)
    w_io_t[...] = dot(w_out[...], wi, 0, 1).astype(BF)
    for copy in copies:
        copy.wait()


def mix_kernel(msg, own_part, m_h, part, node, wide, m, sems):
    feat = lax.axis_index("feat")
    rows = own_part.shape[1]
    count = HALF_DEPTH * LANES
    halo = rows + feat * count
    starts = [halo + k for k in chunks(count)]
    copies = row_copies(m_h, m, sems, starts, CHUNK, chunks(count))
    for copy in copies:
        copy.start()
    wide[...] = msg[...].astype(F32)
    for k in range(2):
        part[:, rows + k * LANES : rows + (k + 1) * LANES] = (
            wide[peer_rows(HALF_DEPTH + k), :].T.astype(BF)
        )
    lists = wide[peer_rows(HALF_DEPTH + 2), :].T
    n = node.shape[0]
    node[...] = ((lists[:n, :] - 1.0) * 32.0 + lists[n : 2 * n, :]).astype(I32)
    got = jnp.concatenate([wide[peer_rows(k), :].T for k in range(HALF_DEPTH)], axis=1).astype(BF)
    acc = own_part[...]
    for k, copy in zip(chunks(count), copies):
        copy.wait()
        acc = acc + dot(got[:, k : k + CHUNK], m[k : k + CHUNK, :])
    part[:, :rows] = acc.astype(BF)


def site_kernel(node, s):
    degree = node.shape[0] // SLOTS
    tiles = [[node[k * degree + j : k * degree + j + 1, :] for j in range(degree)] for k in range(SLOTS)]
    build_counts(s, tiles, s.shape[0])


def node_kernel(
    part,
    other,
    ginc,
    m_h,
    s,
    w_cat_h,
    w_cat_t,
    w_ho_h,
    w_ho_t,
    w_io_h,
    w_io_t,
    msg,
    own,
    agg_out,
    slope_s,
    wide,
    m,
    sems,
    w_cat,
    w_ho,
    w_io,
    w_sems,
):
    feat = lax.axis_index("feat")
    variables, rows = ginc.shape
    late = [
        pltpu.make_async_copy(a, b, w_sems.at[k])
        for k, (a, b) in enumerate(((w_ho_h, w_ho), (w_cat_h, w_cat), (w_io_h, w_io)))
    ]
    for copy in late:
        copy.start()
    copies = row_copies(m_h, m, sems, [rows + k for k in chunks(m.shape[0])], CHUNK, chunks(m.shape[0]))
    for copy in copies:
        copy.start()
    gi = ginc[...]
    agg = (part[:, :rows].astype(F32) + other[:, :rows].astype(F32)).astype(BF)
    pre = dot(w_cat_t[...], jnp.concatenate([gi, agg], axis=0))
    sig = 1.0 / (1.0 + jnp.exp(-pre))
    hidden = (pre * sig).astype(BF)
    slope_s[...] = sig * (1.0 + pre * (1.0 - sig))
    readout = (dot(w_ho_t[...], hidden) + dot(w_io_t[...], gi)).astype(BF)
    values = dot(readout, s[...])
    mine = part[:, rows:].astype(F32)
    theirs = other[:, rows:].astype(F32)
    first = jnp.where(feat == 0, mine, theirs)
    second = jnp.where(feat == 0, theirs, mine)
    diff = (values - jnp.concatenate([first, second], axis=1)).astype(BF)
    d = dot(diff, s[...], 1, 1).astype(BF)
    for copy in late:
        copy.wait()
    inner = (dot(w_ho[...], d) * slope_s[...]).astype(BF)
    n = variables // 2
    cols = pl.ds(pl.multiple_of(feat * n, n), n)
    agg_cols = pl.ds(pl.multiple_of(variables + feat * n, n), n)
    both = dot(jnp.concatenate([w_cat[cols, :], w_cat[agg_cols, :]], axis=0), inner)
    agg_grad = both[n:, :].T.astype(BF)
    agg_out[...] = agg_grad
    own[...] = dot(w_io[cols, :], d) + both[:n, :]
    site_rows = values.T
    for k in range(SLOTS):
        wide[peer_rows(HALF_DEPTH + k), :] = site_rows[k * LANES : (k + 1) * LANES, :]
    for copy in copies:
        copy.wait()
    count = HALF_DEPTH * LANES
    low = dot(m[:count, :], agg_grad)
    high = dot(m[count:, :], agg_grad)
    halo = jnp.concatenate([low, high], axis=1)
    for k in range(HALF_DEPTH):
        wide[peer_rows(k), :] = halo[k * LANES : (k + 1) * LANES, :]
    msg[...] = wide[...].astype(BF)


def scatter_kernel(
    edges, target, send, own_in, agg_grad, m_h, g_h, near, target_col, send_out, own, g, m, sems, m_sem
):
    load = pltpu.make_async_copy(m_h.at[pl.ds(0, m.shape[0]), :], m, m_sem)
    load.start()
    send_out[...] = send[...]
    target_col[...] = jnp.broadcast_to(target[...], (8, target.shape[1])).T[:, :1]
    e = edges[...]
    columns = jnp.concatenate([e, e], axis=0).T
    block = g.shape[0] // sems.shape[0]
    copies = row_copies(g, g_h, sems, range(0, g.shape[0], block), block)
    build_rows(g, columns, g.shape[0], e.shape[0], block, after=lambda n: copies[n].start())
    build_rows(near, columns - g.shape[1], near.shape[0], e.shape[0], block)
    load.wait()
    own[...] = own_in[...] + dot(m[...], agg_grad[...]).T
    for copy in copies:
        copy.wait()


def finish_kernel(
    msg, send, own, target, near, g_h, out_h, pred, wide, r, g, out, in_sems, out_sems, *, degree
):
    far = g.shape[1]
    piece = far // PIECES
    spans = [(k, piece) for k in range(0, far, piece)] + [(far, near.shape[1])]
    spans = [pl.ds(*span) for span in spans]
    loads = [
        pltpu.make_async_copy(g_h.at[:, at], g.at[:, at], in_sems.at[k])
        for k, at in enumerate(spans[:-1])
    ]
    stores = [
        pltpu.make_async_copy(out.at[:, at], out_h.at[:, at], out_sems.at[k])
        for k, at in enumerate(spans)
    ]
    for load in loads:
        load.start()
    depth = send.shape[0]
    build_counts(r, [[send[k : k + 1, :]] for k in range(depth)], r.shape[0], unroll=2)
    wide[...] = msg[...].astype(F32)
    back = jnp.concatenate([wide[peer_rows(k), :] for k in range(HALF_DEPTH)], axis=0).astype(BF)
    count = back.shape[0]
    n = own.shape[0]
    low = dot(r[:, :count], back).T
    high = dot(r[:, count:], back).T
    grad = ((own[...] + low[:n, :] + high[n:, :]) * (1.0 / degree)).astype(BF)
    slots = [wide[peer_rows(HALF_DEPTH + k), :] for k in range(SLOTS)]
    pick = jnp.where(target[...] == iota((target.shape[0], SLOTS * LANES), 1), 1.0, 0.0).astype(BF)
    pred[...] = dot(pick, jnp.concatenate(slots, axis=0).astype(BF)).astype(BF)
    out[:, far:] = dot(grad, near[...])
    stores[-1].start()
    for at, load, store in zip(spans, loads, stores):
        load.wait()
        out[:, at] = dot(grad, g[:, at])
        store.start()
    for store in stores:
        store.wait()


FULL = pl.BlockSpec(memory_space=pltpu.VMEM)
HBM = pl.BlockSpec(memory_space=pl.ANY)
STAY, LEAVE, COPY = "stay", "leave", "copy"


def vmem(x):
    return pltpu.with_memory_space_constraint(x, pltpu.VMEM)


def dma(n):
    return pltpu.SemaphoreType.DMA((n,))


def call(kernel, outs, args, scratch=(), far=(), name=None):
    return pl.pallas_call(
        kernel,
        out_shape=[
            pltpu.VMEM(s, t) if where == STAY else jax.ShapeDtypeStruct(s, t) for s, t, where in outs
        ],
        in_specs=[HBM if k in far else FULL for k in range(len(args))],
        out_specs=[HBM if where == COPY else FULL for _, _, where in outs],
        scratch_shapes=list(scratch),
        name=name,
    )(*args)


def exchange(msg, domains):
    x = msg.reshape(domains, ROWS // 4, 4, msg.shape[1])
    x = lax.all_to_all(x, "dom", split_axis=0, concat_axis=0, tiled=True)
    return x.reshape(msg.shape)


def local(
    increments,
    w_in,
    w_node1,
    w_node2,
    w_out,
    grid_edges,
    mesh_edges,
    mesh_mask,
    send_rows,
    site_owner,
    site_nodes,
    site_obs,
):
    domains = lax.axis_size("dom")
    grid_rows, variables = increments.shape
    mesh_rows = mesh_edges.shape[0]
    inner = w_node2.shape[0]
    site_count = site_obs.shape[0]
    rows = domains * ROWS
    degree = grid_edges.shape[1]
    n = variables // 2
    neighbours = mesh_rows + 2 * HALF_DEPTH * domains
    wide = pltpu.VMEM((rows, variables), F32)
    grid_t = grid_edges.T
    send_t = send_rows[0].T
    small = (send_t, site_owner.T, site_nodes.T, site_obs)
    msg, ginc, target = call(
        encode_kernel,
        [
            ((rows, variables), BF, LEAVE),
            ((variables, mesh_rows), BF, STAY),
            ((1, site_count), I32, LEAVE),
        ],
        (increments, grid_t, *small),
        [
            pltpu.VMEM((grid_rows, mesh_rows), BF),
            pltpu.VMEM((mesh_rows, HALF_DEPTH * domains), BF),
            wide,
            pltpu.VMEM((grid_rows, variables), BF),
            pltpu.SemaphoreType.DMA,
            *[pltpu.VMEM(v.shape, v.dtype) for v in small],
            dma(len(small)),
        ],
        far=(0, 2, 3, 4, 5),
        name="encode",
    )
    m, own_part, *weights = call(
        prepare_kernel,
        [
            ((neighbours, mesh_rows), BF, COPY),
            ((variables, mesh_rows), F32, STAY),
            ((2 * variables, inner), BF, LEAVE),
            ((inner, 2 * variables), BF, STAY),
            ((inner, variables), BF, LEAVE),
            ((variables, inner), BF, STAY),
            ((variables, variables), BF, LEAVE),
            ((variables, variables), BF, STAY),
        ],
        (mesh_edges.T, mesh_mask.T, vmem(ginc), w_in, w_node1, w_node2, w_out),
        [pltpu.VMEM((neighbours, mesh_rows), BF), dma(neighbours // CHUNK)],
        name="prepare",
    )
    got = exchange(msg, domains)
    part, node = call(
        mix_kernel,
        [
            ((variables, mesh_rows + 2 * LANES), BF, STAY),
            ((SLOTS * site_nodes.shape[1], LANES), I32, STAY),
        ],
        (vmem(got), vmem(own_part), m),
        [
            wide,
            pltpu.VMEM((HALF_DEPTH * domains, mesh_rows), BF),
            dma(HALF_DEPTH * domains // CHUNK),
        ],
        far=(2,),
        name="mix",
    )
    other = lax.ppermute(part, "feat", SWAP)
    (sites,) = call(
        site_kernel,
        [((mesh_rows, SLOTS * domains), BF, STAY)],
        (vmem(node),),
        name="sites",
    )
    back, own, agg_grad = call(
        node_kernel,
        [
            ((rows, variables), BF, LEAVE),
            ((n, mesh_rows), F32, LEAVE),
            ((mesh_rows, n), BF, LEAVE),
        ],
        (
            vmem(part),
            vmem(other),
            vmem(ginc),
            m,
            vmem(sites),
            *[vmem(w) if k % 2 else w for k, w in enumerate(weights)],
        ),
        [
            pltpu.VMEM((inner, mesh_rows), F32),
            wide,
            pltpu.VMEM((neighbours - mesh_rows, mesh_rows), BF),
            dma((neighbours - mesh_rows) // CHUNK),
            *[pltpu.VMEM(w.shape, BF) for w in (weights[0], weights[2], weights[4])],
            dma(3),
        ],
        far=(3, 5, 7, 9),
        name="node",
    )
    got_back = exchange(back, domains)
    near_cells = 3 * CHUNK // 2
    far = grid_rows - near_cells
    g, near, target_col, send_near, own = call(
        scatter_kernel,
        [
            ((mesh_rows, far), BF, COPY),
            ((mesh_rows, near_cells), BF, STAY),
            ((site_count, 1), I32, STAY),
            (send_t.shape, I32, STAY),
            ((n, mesh_rows), F32, STAY),
        ],
        (grid_t, target, send_t, own, agg_grad, m),
        [
            pltpu.VMEM((mesh_rows, far), BF),
            pltpu.VMEM((mesh_rows, mesh_rows), BF),
            dma(8),
            pltpu.SemaphoreType.DMA,
        ],
        far=(5,),
        name="scatter",
    )

    def finish(*refs):
        finish_kernel(*refs, degree=degree)

    grad, site_pred = call(
        finish,
        [((n, grid_rows), F32, COPY), ((site_count, variables), BF, LEAVE)],
        (vmem(got_back), vmem(send_near), vmem(own), vmem(target_col), vmem(near), g),
        [
            wide,
            pltpu.VMEM((mesh_rows, 2 * HALF_DEPTH * domains), BF),
            pltpu.VMEM((mesh_rows, far), BF),
            pltpu.VMEM((n, grid_rows), F32),
            dma(PIECES),
            dma(PIECES + 1),
        ],
        far=(5,),
        name="finish",
    )
    return (grad.T, site_pred)


def solution(mesh):
    return jax.shard_map(
        local,
        mesh=mesh,
        in_specs=(
            P("dom", None),
            P(),
            P(),
            P(),
            P(),
            P("dom", None),
            P("dom", None),
            P("dom", None),
            P("dom", None, None),
            P("dom", None),
            P("dom", None),
            P("dom", None),
        ),
        out_specs=(P("dom", "feat"), P("dom", None)),
        check_vma=False,
    )
```

```python
import jax
import jax.numpy as jnp
from jax import lax
from jax.experimental import pallas as pl
from jax.experimental.pallas import tpu as pltpu
from jax.sharding import PartitionSpec as P

BF = jnp.bfloat16
F32 = jnp.float32
I16 = jnp.int16
I32 = jnp.int32
LANES = 128
HALF_DEPTH = 8
SLOTS = 4
ROWS = HALF_DEPTH + SLOTS
SWAP = [(0, 1), (1, 0)]
PIECES = 2
CHUNK = 512


def dot(a, b, ca=1, cb=0):
    return lax.dot_general(a, b, (((ca,), (cb,)), ((), ())), preferred_element_type=F32)


def iota(shape, axis):
    return lax.broadcasted_iota(I32, shape, axis)


def eq_bf16(a, b):
    return jnp.where(a == b, jnp.asarray(1, BF), jnp.asarray(0, BF))


def build_counts(dst, tiles, height, lane0=0, row0=0, sub=16, unroll=4):
    cols = [[jnp.broadcast_to(r, (sub, LANES)).astype(I16) for r in rows] for rows in tiles]
    start = (iota((sub, LANES), 0) + row0).astype(I16)

    def body(i, at):
        s = pl.multiple_of(row0 + i * sub, sub)
        for t, rows in enumerate(cols):
            acc = eq_bf16(rows[0], at)
            for r in rows[1:]:
                acc = acc + eq_bf16(r, at)
            dst[pl.ds(s, sub), lane0 + t * LANES : lane0 + (t + 1) * LANES] = acc
        return at + jnp.asarray(sub, I16)

    lax.fori_loop(0, height // sub, body, start, unroll=unroll)


def build_rows(dst, index, rows, degree, block=128, unroll=2, after=None):
    start = iota((block, LANES), 1).astype(I16)
    for n, s in enumerate(range(0, rows, block)):
        cols = [
            jnp.broadcast_to(index[s : s + block, k : k + 1], (block, LANES)).astype(I16)
            for k in range(degree)
        ]

        def body(w, at, s=s, cols=cols):
            acc = eq_bf16(cols[0], at)
            for c in cols[1:]:
                acc = acc + eq_bf16(c, at)
            dst[s : s + block, pl.ds(pl.multiple_of(w * LANES, LANES), LANES)] = acc
            return at + jnp.asarray(LANES, I16)

        lax.fori_loop(0, dst.shape[1] // LANES, body, start, unroll=unroll)
        if after is not None:
            after(n)


def row_copies(src, dst, sems, starts, size, targets=None):
    targets = starts if targets is None else targets
    return [
        pltpu.make_async_copy(src.at[pl.ds(a, size), :], dst.at[pl.ds(b, size), :], sems.at[k])
        for k, (a, b) in enumerate(zip(starts, targets))
    ]


def chunks(total):
    return range(0, total, CHUNK)


def lane_tiles(rows, first=0, last=None):
    last = rows.shape[1] // LANES if last is None else last
    return [
        [rows[k : k + 1, t * LANES : (t + 1) * LANES] for k in range(rows.shape[0])]
        for t in range(first, last)
    ]


def peer_rows(k):
    return pl.ds(k, LANES, stride=ROWS)


def encode_kernel(
    inc_h, edges, *refs
):
    small_h, (msg, ginc, target, g, r, wide, inc, sem), (*small, sems) = refs[:4], refs[4:12], refs[12:]
    send, owner, nodes, obs = small
    feat = lax.axis_index("feat")
    load = pltpu.make_async_copy(inc_h, inc, sem)
    late = [pltpu.make_async_copy(a, b, sems.at[k]) for k, (a, b) in enumerate(zip(small_h, small))]
    for copy in late:
        copy.start()
    load.start()
    build_counts(g, lane_tiles(edges[...]), inc.shape[0], unroll=8)
    for copy in late:
        copy.wait()
    picked = jnp.where(feat == 0, send[:HALF_DEPTH, :], send[HALF_DEPTH:, :])
    build_counts(r, [[picked[k : k + 1, :]] for k in range(HALF_DEPTH)], r.shape[0])
    sites = owner.shape[1]
    own = owner[...]
    member = jnp.where(iota((LANES, sites), 0) == own, 1.0, 0.0)
    member_b = member.astype(BF)
    upper = jnp.where(iota((sites, sites), 0) < iota((sites, sites), 1), 1.0, 0.0).astype(BF)
    rank = jnp.sum(dot(member_b, upper) * member, axis=0, keepdims=True)
    target[...] = rank.astype(I32) * LANES + own
    for k in range(2):
        slot = (2 * feat + k).astype(F32)
        wide[peer_rows(HALF_DEPTH + k), :] = dot(
            jnp.where(rank == slot, member, 0.0).astype(BF), obs[...]
        )
    n = nodes[...]
    high = ((n >> 5) + 1).astype(F32)
    low = (n & 31).astype(F32)
    lists = [jnp.where(rank == float(k), v, 0.0) for v in (high, low) for k in range(SLOTS)]
    lists.append(jnp.zeros((LANES - 2 * SLOTS * n.shape[0], sites), F32))
    listed = jnp.concatenate(lists, axis=0).astype(BF)
    wide[peer_rows(HALF_DEPTH + 2), :] = dot(member_b, listed, 1, 1)
    wide[peer_rows(HALF_DEPTH + 3), :] = jnp.zeros((LANES, LANES), F32)
    load.wait()
    mean = (dot(inc[...], g[...], 0, 0) * (1.0 / edges.shape[0])).astype(BF)
    ginc[...] = mean
    out = dot(mean, r[...])
    for k in range(HALF_DEPTH):
        wide[peer_rows(k), :] = out[:, k * LANES : (k + 1) * LANES].T
    msg[...] = wide[...].astype(BF)


def prepare_kernel(
    edges, mask, ginc, w_in, w_node1, w_node2, w_out, m_h, part, w_cat, w_cat_t, w_ho, w_ho_t, w_io, w_io_t, m, sems
):
    rows = edges.shape[1]
    e = edges[...]
    h = e - rows
    r = h & 15
    at = jnp.where(mask[...] > 0, jnp.where(e < rows, e, rows + r * LANES + (h >> 4)), -1)
    tiles = lane_tiles(at)
    copies = row_copies(m, m_h, sems, chunks(m.shape[0]), CHUNK)
    for row0, copy in zip(chunks(m.shape[0]), copies):
        for first in range(0, len(tiles), 4):
            build_counts(m, tiles[first : first + 4], CHUNK, first * LANES, row0)
        copy.start()
    half = rows // 2
    own = pl.ds(pl.multiple_of(lax.axis_index("feat") * half, half), half)
    part[...] = dot(ginc[:, own], m[own, :])
    width = w_in.shape[1]
    variables = w_in.shape[0]
    wi = w_in[...]
    for k in range(2):
        w1 = w_node1[k * width : (k + 1) * width, :]
        w_cat[k * variables : (k + 1) * variables, :] = dot(wi, w1).astype(BF)
        w_cat_t[:, k * variables : (k + 1) * variables] = dot(w1, wi, 0, 1).astype(BF)
    w_ho[...] = dot(w_node2[...], w_out[...]).astype(BF)
    w_ho_t[...] = dot(w_out[...], w_node2[...], 0, 1).astype(BF)
    w_io[...] = dot(wi, w_out[...]).astype(BF)
    w_io_t[...] = dot(w_out[...], wi, 0, 1).astype(BF)
    for copy in copies:
        copy.wait()


def mix_kernel(msg, own_part, m_h, part, node, wide, m, sems):
    feat = lax.axis_index("feat")
    rows = own_part.shape[1]
    count = HALF_DEPTH * LANES
    halo = rows + feat * count
    starts = [halo + k for k in chunks(count)]
    copies = row_copies(m_h, m, sems, starts, CHUNK, chunks(count))
    for copy in copies:
        copy.start()
    wide[...] = msg[...].astype(F32)
    for k in range(2):
        part[:, rows + k * LANES : rows + (k + 1) * LANES] = (
            wide[peer_rows(HALF_DEPTH + k), :].T.astype(BF)
        )
    lists = wide[peer_rows(HALF_DEPTH + 2), :].T
    n = node.shape[0]
    node[...] = ((lists[:n, :] - 1.0) * 32.0 + lists[n : 2 * n, :]).astype(I32)
    got = jnp.concatenate([wide[peer_rows(k), :].T for k in range(HALF_DEPTH)], axis=1).astype(BF)
    acc = own_part[...]
    for k, copy in zip(chunks(count), copies):
        copy.wait()
        acc = acc + dot(got[:, k : k + CHUNK], m[k : k + CHUNK, :])
    part[:, :rows] = acc.astype(BF)


def site_kernel(node, s):
    degree = node.shape[0] // SLOTS
    tiles = [[node[k * degree + j : k * degree + j + 1, :] for j in range(degree)] for k in range(SLOTS)]
    build_counts(s, tiles, s.shape[0])


def node_kernel(
    part,
    other,
    ginc,
    m_h,
    s,
    w_cat_h,
    w_cat_t,
    w_ho_h,
    w_ho_t,
    w_io_h,
    w_io_t,
    msg,
    own,
    agg_out,
    slope_s,
    wide,
    m,
    sems,
    w_cat,
    w_ho,
    w_io,
    w_sems,
):
    feat = lax.axis_index("feat")
    variables, rows = ginc.shape
    late = [
        pltpu.make_async_copy(a, b, w_sems.at[k])
        for k, (a, b) in enumerate(((w_ho_h, w_ho), (w_cat_h, w_cat), (w_io_h, w_io)))
    ]
    for copy in late:
        copy.start()
    copies = row_copies(m_h, m, sems, [rows + k for k in chunks(m.shape[0])], CHUNK, chunks(m.shape[0]))
    for copy in copies:
        copy.start()
    gi = ginc[...]
    agg = (part[:, :rows].astype(F32) + other[:, :rows].astype(F32)).astype(BF)
    pre = dot(w_cat_t[...], jnp.concatenate([gi, agg], axis=0))
    sig = 1.0 / (1.0 + jnp.exp(-pre))
    hidden = (pre * sig).astype(BF)
    slope_s[...] = sig * (1.0 + pre * (1.0 - sig))
    readout = (dot(w_ho_t[...], hidden) + dot(w_io_t[...], gi)).astype(BF)
    values = dot(readout, s[...])
    mine = part[:, rows:].astype(F32)
    theirs = other[:, rows:].astype(F32)
    first = jnp.where(feat == 0, mine, theirs)
    second = jnp.where(feat == 0, theirs, mine)
    diff = (values - jnp.concatenate([first, second], axis=1)).astype(BF)
    d = dot(diff, s[...], 1, 1).astype(BF)
    for copy in late:
        copy.wait()
    inner = (dot(w_ho[...], d) * slope_s[...]).astype(BF)
    n = variables // 2
    cols = pl.ds(pl.multiple_of(feat * n, n), n)
    agg_cols = pl.ds(pl.multiple_of(variables + feat * n, n), n)
    both = dot(jnp.concatenate([w_cat[cols, :], w_cat[agg_cols, :]], axis=0), inner)
    agg_grad = both[n:, :].T.astype(BF)
    agg_out[...] = agg_grad
    own[...] = dot(w_io[cols, :], d) + both[:n, :]
    site_rows = values.T
    for k in range(SLOTS):
        wide[peer_rows(HALF_DEPTH + k), :] = site_rows[k * LANES : (k + 1) * LANES, :]
    for copy in copies:
        copy.wait()
    count = HALF_DEPTH * LANES
    low = dot(m[:count, :], agg_grad)
    high = dot(m[count:, :], agg_grad)
    halo = jnp.concatenate([low, high], axis=1)
    for k in range(HALF_DEPTH):
        wide[peer_rows(k), :] = halo[k * LANES : (k + 1) * LANES, :]
    msg[...] = wide[...].astype(BF)


def scatter_kernel(
    edges, target, send, own_in, agg_grad, m_h, g_h, near, target_col, send_out, own, g, m, sems, m_sem
):
    load = pltpu.make_async_copy(m_h.at[pl.ds(0, m.shape[0]), :], m, m_sem)
    load.start()
    send_out[...] = send[...]
    target_col[...] = jnp.broadcast_to(target[...], (8, target.shape[1])).T[:, :1]
    e = edges[...]
    columns = jnp.concatenate([e, e], axis=0).T
    block = g.shape[0] // sems.shape[0]
    copies = row_copies(g, g_h, sems, range(0, g.shape[0], block), block)
    build_rows(g, columns, g.shape[0], e.shape[0], block, after=lambda n: copies[n].start())
    build_rows(near, columns - g.shape[1], near.shape[0], e.shape[0], block)
    load.wait()
    own[...] = own_in[...] + dot(m[...], agg_grad[...]).T
    for copy in copies:
        copy.wait()


def finish_kernel(
    msg, send, own, target, near, g_h, out_h, pred, wide, r, g, out, in_sems, out_sems, *, degree
):
    far = g.shape[1]
    piece = far // PIECES
    spans = [(k, piece) for k in range(0, far, piece)] + [(far, near.shape[1])]
    spans = [pl.ds(*span) for span in spans]
    loads = [
        pltpu.make_async_copy(g_h.at[:, at], g.at[:, at], in_sems.at[k])
        for k, at in enumerate(spans[:-1])
    ]
    stores = [
        pltpu.make_async_copy(out.at[:, at], out_h.at[:, at], out_sems.at[k])
        for k, at in enumerate(spans)
    ]
    for load in loads:
        load.start()
    depth = send.shape[0]
    build_counts(r, [[send[k : k + 1, :]] for k in range(depth)], r.shape[0], unroll=8)
    wide[...] = msg[...].astype(F32)
    back = jnp.concatenate([wide[peer_rows(k), :] for k in range(HALF_DEPTH)], axis=0).astype(BF)
    count = back.shape[0]
    n = own.shape[0]
    low = dot(r[:, :count], back).T
    high = dot(r[:, count:], back).T
    grad = ((own[...] + low[:n, :] + high[n:, :]) * (1.0 / degree)).astype(BF)
    slots = [wide[peer_rows(HALF_DEPTH + k), :] for k in range(SLOTS)]
    pick = jnp.where(target[...] == iota((target.shape[0], SLOTS * LANES), 1), 1.0, 0.0).astype(BF)
    pred[...] = dot(pick, jnp.concatenate(slots, axis=0).astype(BF)).astype(BF)
    out[:, far:] = dot(grad, near[...])
    stores[-1].start()
    for at, load, store in zip(spans, loads, stores):
        load.wait()
        out[:, at] = dot(grad, g[:, at])
        store.start()
    for store in stores:
        store.wait()


FULL = pl.BlockSpec(memory_space=pltpu.VMEM)
HBM = pl.BlockSpec(memory_space=pl.ANY)
STAY, LEAVE, COPY = "stay", "leave", "copy"


def vmem(x):
    return pltpu.with_memory_space_constraint(x, pltpu.VMEM)


def dma(n):
    return pltpu.SemaphoreType.DMA((n,))


def call(kernel, outs, args, scratch=(), far=(), name=None):
    return pl.pallas_call(
        kernel,
        out_shape=[
            pltpu.VMEM(s, t) if where == STAY else jax.ShapeDtypeStruct(s, t) for s, t, where in outs
        ],
        in_specs=[HBM if k in far else FULL for k in range(len(args))],
        out_specs=[HBM if where == COPY else FULL for _, _, where in outs],
        scratch_shapes=list(scratch),
        name=name,
    )(*args)


def exchange(msg, domains):
    x = msg.reshape(domains, ROWS // 4, 4, msg.shape[1])
    x = lax.all_to_all(x, "dom", split_axis=0, concat_axis=0, tiled=True)
    return x.reshape(msg.shape)


def local(
    increments,
    w_in,
    w_node1,
    w_node2,
    w_out,
    grid_edges,
    mesh_edges,
    mesh_mask,
    send_rows,
    site_owner,
    site_nodes,
    site_obs,
):
    domains = lax.axis_size("dom")
    grid_rows, variables = increments.shape
    mesh_rows = mesh_edges.shape[0]
    inner = w_node2.shape[0]
    site_count = site_obs.shape[0]
    rows = domains * ROWS
    degree = grid_edges.shape[1]
    n = variables // 2
    neighbours = mesh_rows + 2 * HALF_DEPTH * domains
    wide = pltpu.VMEM((rows, variables), F32)
    grid_t = grid_edges.T
    send_t = send_rows[0].T
    small = (send_t, site_owner.T, site_nodes.T, site_obs)
    msg, ginc, target = call(
        encode_kernel,
        [
            ((rows, variables), BF, LEAVE),
            ((variables, mesh_rows), BF, STAY),
            ((1, site_count), I32, LEAVE),
        ],
        (increments, grid_t, *small),
        [
            pltpu.VMEM((grid_rows, mesh_rows), BF),
            pltpu.VMEM((mesh_rows, HALF_DEPTH * domains), BF),
            wide,
            pltpu.VMEM((grid_rows, variables), BF),
            pltpu.SemaphoreType.DMA,
            *[pltpu.VMEM(v.shape, v.dtype) for v in small],
            dma(len(small)),
        ],
        far=(0, 2, 3, 4, 5),
        name="encode",
    )
    m, own_part, *weights = call(
        prepare_kernel,
        [
            ((neighbours, mesh_rows), BF, COPY),
            ((variables, mesh_rows), F32, STAY),
            ((2 * variables, inner), BF, LEAVE),
            ((inner, 2 * variables), BF, STAY),
            ((inner, variables), BF, LEAVE),
            ((variables, inner), BF, STAY),
            ((variables, variables), BF, LEAVE),
            ((variables, variables), BF, STAY),
        ],
        (mesh_edges.T, mesh_mask.T, vmem(ginc), w_in, w_node1, w_node2, w_out),
        [pltpu.VMEM((neighbours, mesh_rows), BF), dma(neighbours // CHUNK)],
        name="prepare",
    )
    got = exchange(msg, domains)
    part, node = call(
        mix_kernel,
        [
            ((variables, mesh_rows + 2 * LANES), BF, STAY),
            ((SLOTS * site_nodes.shape[1], LANES), I32, STAY),
        ],
        (vmem(got), vmem(own_part), m),
        [
            wide,
            pltpu.VMEM((HALF_DEPTH * domains, mesh_rows), BF),
            dma(HALF_DEPTH * domains // CHUNK),
        ],
        far=(2,),
        name="mix",
    )
    other = lax.ppermute(part, "feat", SWAP)
    (sites,) = call(
        site_kernel,
        [((mesh_rows, SLOTS * domains), BF, STAY)],
        (vmem(node),),
        name="sites",
    )
    back, own, agg_grad = call(
        node_kernel,
        [
            ((rows, variables), BF, LEAVE),
            ((n, mesh_rows), F32, LEAVE),
            ((mesh_rows, n), BF, LEAVE),
        ],
        (
            vmem(part),
            vmem(other),
            vmem(ginc),
            m,
            vmem(sites),
            *[vmem(w) if k % 2 else w for k, w in enumerate(weights)],
        ),
        [
            pltpu.VMEM((inner, mesh_rows), F32),
            wide,
            pltpu.VMEM((neighbours - mesh_rows, mesh_rows), BF),
            dma((neighbours - mesh_rows) // CHUNK),
            *[pltpu.VMEM(w.shape, BF) for w in (weights[0], weights[2], weights[4])],
            dma(3),
        ],
        far=(3, 5, 7, 9),
        name="node",
    )
    got_back = exchange(back, domains)
    near_cells = 3 * CHUNK // 2
    far = grid_rows - near_cells
    g, near, target_col, send_near, own = call(
        scatter_kernel,
        [
            ((mesh_rows, far), BF, COPY),
            ((mesh_rows, near_cells), BF, STAY),
            ((site_count, 1), I32, STAY),
            (send_t.shape, I32, STAY),
            ((n, mesh_rows), F32, STAY),
        ],
        (grid_t, target, send_t, own, agg_grad, m),
        [
            pltpu.VMEM((mesh_rows, far), BF),
            pltpu.VMEM((mesh_rows, mesh_rows), BF),
            dma(8),
            pltpu.SemaphoreType.DMA,
        ],
        far=(5,),
        name="scatter",
    )

    def finish(*refs):
        finish_kernel(*refs, degree=degree)

    grad, site_pred = call(
        finish,
        [((n, grid_rows), F32, COPY), ((site_count, variables), BF, LEAVE)],
        (vmem(got_back), vmem(send_near), vmem(own), vmem(target_col), vmem(near), g),
        [
            wide,
            pltpu.VMEM((mesh_rows, 2 * HALF_DEPTH * domains), BF),
            pltpu.VMEM((mesh_rows, far), BF),
            pltpu.VMEM((n, grid_rows), F32),
            dma(PIECES),
            dma(PIECES + 1),
        ],
        far=(5,),
        name="finish",
    )
    return (grad.T, site_pred)


def solution(mesh):
    return jax.shard_map(
        local,
        mesh=mesh,
        in_specs=(
            P("dom", None),
            P(),
            P(),
            P(),
            P(),
            P("dom", None),
            P("dom", None),
            P("dom", None),
            P("dom", None, None),
            P("dom", None),
            P("dom", None),
            P("dom", None),
        ),
        out_specs=(P("dom", "feat"), P("dom", None)),
        check_vma=False,
    )
```
